32 devices in a mesh: lat: 16 (over z, x, core), lon: 2 (over y).
Axes of the slice: x: 2, y: 2, z: 4, core: 2. Of those that a mesh axis runs over, the one named last changes fastest.
Arguments:
- elevation: float32 [16, 1024, 1024], P(None, 'lat', 'lon'), may hold values from -6 to 6
- depth: float32 [1024, 1024], P('lat', 'lon'), may hold values from 0.3 to 3
- friction: float32 [1024, 1024], P('lat', 'lon'), may hold values from 0.05 to 1
- land_mask: int32 [1024, 1024], P('lat', 'lon'), may hold values 0 or 1
- order_map: int32 [32], replicated, may hold values from 0 to 31, each once
- legendre: bfloat16 [32, 1024, 2048], P('lon', 'lat'), may hold values from -0.1875 to 0.1875
- load: float32 [2048], replicated, may hold values from 0.25 to 4
Outputs:
- elevation_new: float32 [16, 1024, 1024], P(None, 'lat', 'lon')
- sal: float32 [16, 1024, 1024], P(None, 'lat', 'lon')
- friction_new: float32 [1024, 1024], P('lat', 'lon')
The draws below stay inside these ranges and needn't reach their ends.
Inputs may be any that keep to these rules, and one draw needn't show every extreme that they name: `order_map`: each order 0 to 31 stands in exactly one slot. `land_mask`: 1 marks sea and 0 land.
All inputs are finite; a program needn't handle non-finite values. No bound on the sum of `land_mask` on one device may be relied on, other than what follows from the above.
Results may differ from the reference program's by a relative error of at most 0.0037.
Values may be sent and summed in bfloat16 or wider, within the bound.
A program may use at most 64 MiB of HBM per device.

```python
import math
import jax
import jax.numpy as jnp
from jax import lax

CONSTITUENTS = 8
DEGREES = 2048
SAMPLES = 64
NLAT = 1024
NLON = 1024
ORDERS = 32


def set_ends(array, rng, least, top_value):
    spot = [jax.random.randint(jax.random.fold_in(rng, axis), (), 0, length) for axis, length in enumerate(array.shape)]
    widest = array.shape.index(max(array.shape))
    neighbour = spot[:widest] + [(spot[widest] + 1) % array.shape[widest]] + spot[widest + 1:]
    return array.at[tuple(spot)].set(least).at[tuple(neighbour)].set(top_value)


def block_levels(stream_key, extent, pieces, smallest, largest):
    level, own = 1.0, jax.random.fold_in(stream_key, 6)
    for axis_at, blocks in pieces:
        steps = jnp.exp(jax.random.uniform(jax.random.fold_in(own, axis_at), (blocks,), jnp.float32, smallest / len(pieces), largest / len(pieces)))
        level = level * jnp.repeat(steps, extent[axis_at] // blocks).reshape([-1 if axis == axis_at else 1 for axis in range(len(extent))])
    return level


def normal_values(rng, shape, scale, limit, shards=(), kind=jnp.bfloat16):
    loudness = block_levels(rng, shape, shards, -0.22, 0.18) if shards else 1.0
    entries = jax.random.normal(rng, shape, jnp.float32) * scale * loudness
    return jnp.minimum(jnp.maximum(entries, -limit), limit).astype(kind)


def setup_inputs(seed: int = 0) -> dict:
    streams_of = jax.random.split(jax.random.key(seed), 8)
    return {
        "elevation": normal_values(streams_of[0], (2 * CONSTITUENTS, NLAT, NLON), 1.0, 6.0, ((1, 16), (2, 2)), jnp.float32),
        "depth": jnp.clip(jnp.exp(math.log(3.0) - 2.3025851 * jax.random.uniform(streams_of[1], (NLAT, NLON), jnp.float32) ** block_levels(streams_of[1], (NLAT, NLON), ((0, 16), (1, 2)), -0.2, 0.2)), 0.3, 3.0),
        "friction": jnp.clip(jnp.exp(math.log(1.0) - 2.9957323 * jax.random.uniform(streams_of[2], (NLAT, NLON), jnp.float32) ** block_levels(streams_of[2], (NLAT, NLON), ((0, 16), (1, 2)), -0.2, 0.2)), 0.05, 1.0),
        "land_mask": set_ends((jax.random.randint(streams_of[3], (NLAT, NLON), 0, 5) < 4).astype(jnp.int32), jax.random.fold_in(streams_of[3], 1), 0, 1),
        "order_map": jax.random.permutation(streams_of[4], ORDERS).astype(jnp.int32),
        "legendre": normal_values(streams_of[5], (ORDERS, NLAT, DEGREES), NLAT ** -0.5, 0.1875, ((0, 2), (1, 16))),
        "load": jnp.clip(jnp.exp(jax.random.uniform(streams_of[6], (DEGREES,), jnp.float32, math.log(0.25), math.log(4.0))), 0.25, 4.0),
    }


FREQUENCIES = (1.0, 1.0347, 0.9582, 1.0379, 0.5018, 0.4651, 0.4986, 0.4482)
EQ_AMPS = (0.73, 0.34, 0.14, 0.09, 0.42, 0.3, 0.14, 0.06)
LAT_EDGE = 1.3614
RELAX_RATE = 0.1
BASE_FRICTION = 0.05
DRAG_COEFF = 0.5
SPEED_EPS = 0.001
STEP_TIME = 3.0
PRECISE = lax.Precision.HIGHEST

def fourier_basis(order_map, col_start, lon_cols, lon_count):
    columns = col_start + jnp.arange(lon_cols, dtype=jnp.int32)
    product = order_map[:, None] * columns[None, :] % lon_count
    angles = product.astype(jnp.float32) * (2.0 * math.pi / lon_count)
    scaling = jnp.where(order_map > 0, math.sqrt(2.0 / lon_count), math.sqrt(1.0 / lon_count)).astype(jnp.float32)[:, None]
    harmonics = jnp.stack([jnp.cos(angles) * scaling, jnp.sin(angles) * scaling], axis=1)
    return harmonics.reshape(2 * order_map.shape[0], lon_cols)

def equilibrium(lat_start, lat_rows, col_start, lon_cols, lat_count, lon_count):
    lat_step = 2.0 * LAT_EDGE / lat_count
    lat_offset = jnp.asarray(lat_start).astype(jnp.float32)
    latitude = (-LAT_EDGE + (lat_offset + jnp.arange(lat_rows, dtype=jnp.float32) + 0.5) * lat_step)[:, None]
    columns = jnp.asarray(col_start).astype(jnp.float32) + jnp.arange(lon_cols, dtype=jnp.float32)
    longitude = (columns * (2.0 * math.pi / lon_count))[None, :]
    fields = []
    for member in range(len(EQ_AMPS)):
        if member < 4:
            shape_lat = EQ_AMPS[member] * jnp.cos(latitude) ** 2
            wave_angle = 2.0 * longitude
        else:
            shape_lat = EQ_AMPS[member] * jnp.sin(2.0 * latitude)
            wave_angle = longitude
        fields.append(shape_lat * jnp.cos(wave_angle))
        fields.append(shape_lat * jnp.sin(wave_angle))
    return jnp.stack(fields, axis=0)

def face_flux(depths, drags, diffs, omegas):
    constit = omegas.shape[0]
    pairs = diffs.reshape((constit, 2) + diffs.shape[1:])
    denominator = drags * drags + omegas * omegas * depths * depths
    real_coef = depths * depths * drags / denominator
    imag_coef = depths * depths * depths * omegas / denominator
    flux_real = -(real_coef * pairs[:, 0] - imag_coef * pairs[:, 1])
    flux_imag = -(real_coef * pairs[:, 1] + imag_coef * pairs[:, 0])
    return jnp.stack([flux_real, flux_imag], axis=1).reshape(diffs.shape)

def relax_sweep(padded, elevation, sea_mask, lat_start, lat_count):
    channels, lat_rows, lon_cols = elevation.shape
    surface = padded[:channels]
    sea_depth = padded[channels]
    drag_field = padded[channels + 1]
    lat_step = 2.0 * LAT_EDGE / lat_count
    lat_offset = jnp.asarray(lat_start).astype(jnp.float32)
    cos_center = jnp.cos(-LAT_EDGE + (lat_offset + jnp.arange(lat_rows, dtype=jnp.float32) + 0.5) * lat_step)[:, None]
    cos_face = jnp.cos(-LAT_EDGE + (lat_offset + jnp.arange(lat_rows + 1, dtype=jnp.float32)) * lat_step)[:, None]
    omegas = jnp.asarray(FREQUENCIES, dtype=jnp.float32)[:, None, None]
    east_depth = jnp.sqrt(sea_depth[1:-1, :-1] * sea_depth[1:-1, 1:])
    east_drag = 0.5 * (drag_field[1:-1, :-1] + drag_field[1:-1, 1:])
    east_diff = (surface[:, 1:-1, 1:] - surface[:, 1:-1, :-1]) / cos_center
    north_depth = jnp.sqrt(sea_depth[:-1, 1:-1] * sea_depth[1:, 1:-1])
    north_drag = 0.5 * (drag_field[:-1, 1:-1] + drag_field[1:, 1:-1])
    north_diff = (surface[:, 1:, 1:-1] - surface[:, :-1, 1:-1]) * cos_face
    east_flux = face_flux(east_depth, east_drag, east_diff, omegas)
    north_flux = face_flux(north_depth, north_drag, north_diff, omegas)
    divergence = (east_flux[:, :, 1:] - east_flux[:, :, :-1] + north_flux[:, 1:] - north_flux[:, :-1]) / cos_center
    constit = omegas.shape[0]
    current = elevation.reshape(constit, 2, lat_rows, lon_cols)
    div_pairs = divergence.reshape(constit, 2, lat_rows, lon_cols)
    resid_real = div_pairs[:, 0] + omegas * current[:, 1]
    resid_imag = div_pairs[:, 1] - omegas * current[:, 0]
    residual = jnp.stack([resid_real, resid_imag], axis=1).reshape(channels, lat_rows, lon_cols)
    elevation_new = (elevation - RELAX_RATE * residual) * sea_mask
    east_cell = 0.5 * (east_flux[:, :, 1:] + east_flux[:, :, :-1])
    north_cell = 0.5 * (north_flux[:, 1:] + north_flux[:, :-1])
    return (elevation_new, east_cell, north_cell)

def sample_table():
    sample_time = STEP_TIME * jnp.arange(SAMPLES, dtype=jnp.float32)[:, None]
    omegas = jnp.asarray(FREQUENCIES, dtype=jnp.float32)[None, :]
    phases = sample_time * omegas
    return jnp.stack([jnp.cos(phases), jnp.sin(phases)], axis=2).reshape(SAMPLES, 2 * len(FREQUENCIES))

def reference(elevation, depth, friction, land_mask, order_map, legendre, load):
    channels, lat_count, lon_count = elevation.shape
    slot_count = order_map.shape[0]
    sea_mask = land_mask.astype(jnp.float32)
    masked = (elevation * sea_mask).reshape(channels * lat_count, lon_count)
    harmonics = fourier_basis(order_map, 0, lon_count, lon_count)
    fourier = lax.dot_general(harmonics, masked, (((1,), (1,)), ((), ())), precision=PRECISE, preferred_element_type=jnp.float32)
    fourier = fourier.reshape(slot_count, 2 * channels, lat_count).astype(jnp.bfloat16)

    def one_order(pair):
        tables, values = pair
        coeffs = jnp.dot(values, tables, preferred_element_type=jnp.float32)
        scaled = (coeffs * load[None, :]).astype(jnp.bfloat16)
        return lax.dot_general(scaled, tables, (((1,), (1,)), ((), ())), preferred_element_type=jnp.float32)
    synthesis = lax.map(one_order, (legendre, fourier))
    left_side = synthesis.reshape(2 * slot_count, channels * lat_count)
    sal = lax.dot_general(left_side, harmonics, (((0,), (0,)), ((), ())), precision=PRECISE, preferred_element_type=jnp.float32)
    sal = sal.reshape(channels, lat_count, lon_count)
    equil_tide = equilibrium(0, lat_count, 0, lon_count, lat_count, lon_count)
    surface = elevation - equil_tide - sal
    stacked = jnp.concatenate([surface, (depth * sea_mask)[None], friction[None]], axis=0)
    padded = jnp.pad(stacked, ((0, 0), (1, 1), (0, 0)))
    padded = jnp.concatenate([padded[:, :, -1:], padded, padded[:, :, :1]], axis=2)
    elevation_new, east_cell, north_cell = relax_sweep(padded, elevation, sea_mask, 0, lat_count)
    weights_all = sample_table()

    def add_sample(summed, weights_row):
        east_time = jnp.einsum('c,cjl->jl', weights_row, east_cell, precision=PRECISE)
        north_time = jnp.einsum('c,cjl->jl', weights_row, north_cell, precision=PRECISE)
        speeds = jnp.sqrt(east_time * east_time + north_time * north_time + SPEED_EPS * SPEED_EPS)
        return (summed + speeds, None)
    summed, unused = lax.scan(add_sample, jnp.zeros((lat_count, lon_count), jnp.float32), weights_all)
    friction_new = BASE_FRICTION + DRAG_COEFF * summed / SAMPLES
    return (elevation_new, sal, friction_new)
```

```python
import functools
import math

import jax
import jax.numpy as jnp
from jax import lax
from jax.experimental import pallas as pl
from jax.experimental.pallas import tpu as pltpu
from jax.sharding import PartitionSpec as P

SAMPLES = 64


FREQUENCIES = (1.0, 1.0347, 0.9582, 1.0379, 0.5018, 0.4651, 0.4986, 0.4482)
EQ_AMPS = (0.73, 0.34, 0.14, 0.09, 0.42, 0.3, 0.14, 0.06)
LAT_EDGE = 1.3614
RELAX_RATE = 0.1
BASE_FRICTION = 0.05
DRAG_COEFF = 0.5
SPEED_EPS = 0.001
STEP_TIME = 3.0
PRECISE = lax.Precision.HIGHEST


def with_halo(value, sides, width):
    for axis, dim in sides:
        size, length = (lax.axis_size(axis), value.shape[dim])
        up = [(i, (i + 1) % size) for i in range(size)]
        down = [(j, i) for i, j in up]
        last = lax.slice_in_dim(value, length - width, length, axis=dim)
        initial = lax.slice_in_dim(value, 0, width, axis=dim)
        before = lax.ppermute(last, axis, up)
        after = lax.ppermute(initial, axis, down)
        value = jnp.concatenate([before, value, after], axis=dim)
    return value


def fourier_basis(order_map, col_start, lon_cols, lon_count):
    columns = col_start + jnp.arange(lon_cols, dtype=jnp.int32)
    product = order_map[:, None] * columns[None, :] % lon_count
    angles = product.astype(jnp.float32) * (2.0 * math.pi / lon_count)
    scaling = jnp.where(
        order_map > 0, math.sqrt(2.0 / lon_count), math.sqrt(1.0 / lon_count)
    ).astype(jnp.float32)[:, None]
    harmonics = jnp.stack([jnp.cos(angles) * scaling, jnp.sin(angles) * scaling], axis=1)
    return harmonics.reshape(2 * order_map.shape[0], lon_cols)


def equilibrium(lat_start, lat_rows, col_start, lon_cols, lat_count, lon_count):
    lat_step = 2.0 * LAT_EDGE / lat_count
    lat_offset = jnp.asarray(lat_start).astype(jnp.float32)
    latitude = (
        -LAT_EDGE + (lat_offset + jnp.arange(lat_rows, dtype=jnp.float32) + 0.5) * lat_step
    )[:, None]
    columns = jnp.asarray(col_start).astype(jnp.float32) + jnp.arange(lon_cols, dtype=jnp.float32)
    longitude = (columns * (2.0 * math.pi / lon_count))[None, :]
    fields = []
    for member in range(len(EQ_AMPS)):
        if member < 4:
            shape_lat = EQ_AMPS[member] * jnp.cos(latitude) ** 2
            wave_angle = 2.0 * longitude
        else:
            shape_lat = EQ_AMPS[member] * jnp.sin(2.0 * latitude)
            wave_angle = longitude
        fields.append(shape_lat * jnp.cos(wave_angle))
        fields.append(shape_lat * jnp.sin(wave_angle))
    return jnp.stack(fields, axis=0)


def face_flux(depths, drags, diffs, omegas):
    constit = omegas.shape[0]
    pairs = diffs.reshape((constit, 2) + diffs.shape[1:])
    denominator = drags * drags + omegas * omegas * depths * depths
    real_coef = depths * depths * drags / denominator
    imag_coef = depths * depths * depths * omegas / denominator
    flux_real = -(real_coef * pairs[:, 0] - imag_coef * pairs[:, 1])
    flux_imag = -(real_coef * pairs[:, 1] + imag_coef * pairs[:, 0])
    return jnp.stack([flux_real, flux_imag], axis=1).reshape(diffs.shape)


def relax_sweep(padded, elevation, sea_mask, lat_start, lat_count):
    channels, lat_rows, lon_cols = elevation.shape
    surface = padded[:channels]
    sea_depth = padded[channels]
    drag_field = padded[channels + 1]
    lat_step = 2.0 * LAT_EDGE / lat_count
    lat_offset = jnp.asarray(lat_start).astype(jnp.float32)
    cos_center = jnp.cos(
        -LAT_EDGE + (lat_offset + jnp.arange(lat_rows, dtype=jnp.float32) + 0.5) * lat_step
    )[:, None]
    cos_face = jnp.cos(
        -LAT_EDGE + (lat_offset + jnp.arange(lat_rows + 1, dtype=jnp.float32)) * lat_step
    )[:, None]
    omegas = jnp.asarray(FREQUENCIES, dtype=jnp.float32)[:, None, None]
    east_depth = jnp.sqrt(sea_depth[1:-1, :-1] * sea_depth[1:-1, 1:])
    east_drag = 0.5 * (drag_field[1:-1, :-1] + drag_field[1:-1, 1:])
    east_diff = (surface[:, 1:-1, 1:] - surface[:, 1:-1, :-1]) / cos_center
    north_depth = jnp.sqrt(sea_depth[:-1, 1:-1] * sea_depth[1:, 1:-1])
    north_drag = 0.5 * (drag_field[:-1, 1:-1] + drag_field[1:, 1:-1])
    north_diff = (surface[:, 1:, 1:-1] - surface[:, :-1, 1:-1]) * cos_face
    east_flux = face_flux(east_depth, east_drag, east_diff, omegas)
    north_flux = face_flux(north_depth, north_drag, north_diff, omegas)
    divergence = (
        east_flux[:, :, 1:] - east_flux[:, :, :-1] + north_flux[:, 1:] - north_flux[:, :-1]
    ) / cos_center
    constit = omegas.shape[0]
    current = elevation.reshape(constit, 2, lat_rows, lon_cols)
    div_pairs = divergence.reshape(constit, 2, lat_rows, lon_cols)
    resid_real = div_pairs[:, 0] + omegas * current[:, 1]
    resid_imag = div_pairs[:, 1] - omegas * current[:, 0]
    residual = jnp.stack([resid_real, resid_imag], axis=1).reshape(channels, lat_rows, lon_cols)
    elevation_new = (elevation - RELAX_RATE * residual) * sea_mask
    east_cell = 0.5 * (east_flux[:, :, 1:] + east_flux[:, :, :-1])
    north_cell = 0.5 * (north_flux[:, 1:] + north_flux[:, :-1])
    return (elevation_new, east_cell, north_cell)


def sample_table():
    sample_time = STEP_TIME * jnp.arange(SAMPLES, dtype=jnp.float32)[:, None]
    omegas = jnp.asarray(FREQUENCIES, dtype=jnp.float32)[None, :]
    phases = sample_time * omegas
    return jnp.stack([jnp.cos(phases), jnp.sin(phases)], axis=2).reshape(
        SAMPLES, 2 * len(FREQUENCIES)
    )


def clear_poles(padded, band_count):
    band_index = lax.axis_index("lat")
    row_ids = jnp.arange(padded.shape[1])
    dropped = (row_ids == 0) & (band_index == 0) | (row_ids == padded.shape[1] - 1) & (
        band_index == band_count - 1
    )
    return jnp.where(dropped[None, :, None], 0.0, padded)


GROUPS = 4
MESH = pl.DeviceIdType.MESH


def transform_kernel(
    lat_size,
    lon_size,
    groups,
    part_ref,
    leg_ref,
    load_ref,
    out_ref,
    sector_parts,
    fourier,
    acc,
    first_recv,
    rs_send,
    rs_recv,
    gathered,
    lon_send,
    lon_recv,
    out_send,
    out_recv,
    red_send,
    red_recv,
    gat_send,
    gat_recv,
):
    lat_me = lax.axis_index("lat")
    lon_me = lax.axis_index("lon")
    levels = lat_size.bit_length() - 1
    slots, lat_rows, degrees = leg_ref.shape
    quantities = part_ref.shape[2]
    rows = slots * quantities
    width = degrees // groups
    bits = [(lat_me // 2**k) % 2 for k in range(levels)]
    partners = [lat_me + (1 - 2 * bits[k]) * 2**k for k in range(levels)]
    others = [lax.rem(lon_me + d, lon_size) for d in range(1, lon_size)]
    kept, sent = [0], []
    for k in range(levels):
        half = rows >> (k + 1)
        sent.append(pl.multiple_of(kept[k] + (1 - bits[k]) * half, half))
        kept.append(pl.multiple_of(kept[k] + bits[k] * half, half))

    barrier = pltpu.get_barrier_semaphore()
    for k in range(levels):
        pl.semaphore_signal(
            barrier, inc=1, device_id=(partners[k], lon_me), device_id_type=MESH
        )
    for other in others:
        pl.semaphore_signal(barrier, inc=1, device_id=(lat_me, other), device_id_type=MESH)
    pl.semaphore_wait(barrier, levels + lon_size - 1)

    pending = []

    def send(source, target, send_sem, recv_sem, device):
        copy = pltpu.make_async_remote_copy(
            src_ref=source,
            dst_ref=target,
            send_sem=send_sem,
            recv_sem=recv_sem,
            device_id=device,
            device_id_type=MESH,
        )
        copy.start()
        pending.append(copy)
        return copy

    copies = [
        send(
            part_ref.at[other],
            sector_parts.at[d],
            lon_send.at[d],
            lon_recv.at[d],
            (lat_me, other),
        )
        for d, other in enumerate(others)
    ]
    for copy in copies:
        copy.wait_recv()
    total = part_ref[lon_me]
    for d in range(lon_size - 1):
        total = total + sector_parts[d]
    fourier[...] = total.astype(jnp.bfloat16)

    reducing = {}
    gathering = {}

    def analyse(g):
        @pl.loop(0, slots)
        def _(s):
            acc[g, pl.ds(pl.multiple_of(s * quantities, quantities), quantities), :] = jnp.dot(
                fourier[s],
                leg_ref[s, :, g * width : (g + 1) * width],
                preferred_element_type=jnp.float32,
            )

        reducing[g] = send(
            acc.at[g, pl.ds(sent[0], rows // 2), :],
            first_recv.at[g],
            red_send.at[g, 0],
            red_recv.at[g, 0],
            (partners[0], lon_me),
        )

    def offset_of(k):
        return rows // 2 - (rows >> k)

    def reduce(g, k):
        reducing[g].wait_recv()
        size = rows >> (k + 1)

        def arrived(start, count):
            if k == 0:
                return first_recv[g, pl.ds(start, count), :]
            return rs_recv[g, pl.ds(offset_of(k) + start, count), :].astype(jnp.float32)

        if k < levels - 1:
            half = size // 2
            away = pl.multiple_of((1 - bits[k + 1]) * half, half)
            home = pl.multiple_of(bits[k + 1] * half, half)
            place = pl.ds(offset_of(k + 1), half)
            rs_send[g, place, :] = (
                acc[g, pl.ds(sent[k + 1], half), :] + arrived(away, half)
            ).astype(jnp.bfloat16)
            reducing[g] = send(
                rs_send.at[g, place, :],
                rs_recv.at[g, place, :],
                red_send.at[g, k + 1],
                red_recv.at[g, k + 1],
                (partners[k + 1], lon_me),
            )
            acc[g, pl.ds(kept[k + 1 + 1], half), :] = acc[
                g, pl.ds(kept[k + 1 + 1], half), :
            ] + arrived(home, half)
        else:
            mine = pl.ds(kept[levels], size)
            scale = load_ref[:, g * width : (g + 1) * width]
            gathered[g, mine, :] = ((acc[g, mine, :] + arrived(0, size)) * scale).astype(
                jnp.bfloat16
            )
            spread(g, levels - 1)

    def spread(g, k):
        held = pl.ds(kept[k + 1], rows >> (k + 1))
        gathering[g] = send(
            gathered.at[g, held, :],
            gathered.at[g, held, :],
            gat_send.at[g, k],
            gat_recv.at[g, k],
            (partners[k], lon_me),
        )

    def synthesise(g):
        @pl.loop(0, slots)
        def _(s):
            part = lax.dot_general(
                gathered[g, pl.ds(pl.multiple_of(s * quantities, quantities), quantities), :],
                leg_ref[s, :, g * width : (g + 1) * width],
                (((1,), (1,)), ((), ())),
                preferred_element_type=jnp.float32,
            )
            if g == 0:
                out_ref[lon_me * slots + s] = part
            else:
                out_ref[lon_me * slots + s] = out_ref[lon_me * slots + s] + part

    def gather(g, k):
        gathering[g].wait_recv()
        if k > 0:
            spread(g, k - 1)
        else:
            synthesise(g)

    for wave in range(groups + 2 * levels):
        for g in range(groups):
            stage = wave - g
            if stage == 0:
                analyse(g)
            elif 1 <= stage <= levels:
                reduce(g, stage - 1)
            elif levels < stage <= 2 * levels:
                gather(g, 2 * levels - stage)

    block = out_ref.at[pl.ds(lon_me * slots, slots)]
    copies = [
        send(block, block, out_send.at[d], out_recv.at[d], (lat_me, other))
        for d, other in enumerate(others)
    ]
    for copy in copies:
        copy.wait_recv()
    for copy in pending:
        copy.wait_send()


def transform(parts, legendre, load, lat_size, lon_size):
    slots, lat_rows, degrees = legendre.shape
    quantities = parts.shape[2]
    rows = slots * quantities
    groups = GROUPS
    width = degrees // groups
    levels = lat_size.bit_length() - 1
    vmem = pl.BlockSpec(memory_space=pltpu.VMEM)
    dma = pltpu.SemaphoreType.DMA
    flops = 4 * rows * lat_rows * degrees
    return pl.pallas_call(
        functools.partial(transform_kernel, lat_size, lon_size, groups),
        out_shape=jax.ShapeDtypeStruct((lon_size * slots, quantities, lat_rows), jnp.float32),
        in_specs=[vmem] * 3,
        out_specs=vmem,
        scratch_shapes=[
            pltpu.VMEM((lon_size - 1, slots, quantities, lat_rows), jnp.float32),
            pltpu.VMEM((slots, quantities, lat_rows), jnp.bfloat16),
            pltpu.VMEM((groups, rows, width), jnp.float32),
            pltpu.VMEM((groups, rows // 2, width), jnp.float32),
            pltpu.VMEM((groups, rows // 2, width), jnp.bfloat16),
            pltpu.VMEM((groups, rows // 2, width), jnp.bfloat16),
            pltpu.VMEM((groups, rows, width), jnp.bfloat16),
            dma((lon_size - 1,)),
            dma((lon_size - 1,)),
            dma((lon_size - 1,)),
            dma((lon_size - 1,)),
            dma((groups, levels)),
            dma((groups, levels)),
            dma((groups, levels)),
            dma((groups, levels)),
        ],
        compiler_params=pltpu.CompilerParams(
            collective_id=0, has_side_effects=True, vmem_limit_bytes=40 * 1024 * 1024
        ),
        cost_estimate=pl.CostEstimate(
            flops=flops, bytes_accessed=2 * slots * lat_rows * degrees, transcendentals=0
        ),
    )(parts, legendre, load[None, :])


def on_device(elevation, depth, friction, land_mask, order_map, legendre, load):
    channels, lat_rows, lon_cols = elevation.shape
    slot_count = legendre.shape[0]
    band_count = lax.axis_size("lat")
    sector_count = lax.axis_size("lon")
    lat_count = lat_rows * band_count
    lon_count = lon_cols * sector_count
    lat_start = lax.axis_index("lat") * lat_rows
    col_start = lax.axis_index("lon") * lon_cols
    sea_mask = land_mask.astype(jnp.float32)
    equil_tide = equilibrium(lat_start, lat_rows, col_start, lon_cols, lat_count, lon_count)
    sea_depth = depth * sea_mask
    base_fields = jnp.concatenate([elevation - equil_tide, sea_depth[None], friction[None]], axis=0)
    base_padded = clear_poles(with_halo(base_fields, (("lat", 1), ("lon", 2)), 1), band_count)
    harmonics = fourier_basis(order_map, col_start, lon_cols, lon_count)
    flat_field = (elevation * sea_mask).reshape(channels * lat_rows, lon_cols)
    part_basis = harmonics
    product = lax.dot_general(
        part_basis,
        flat_field,
        (((1,), (1,)), ((), ())),
        precision=PRECISE,
        preferred_element_type=jnp.float32,
    )
    parts = product.reshape(sector_count, slot_count, 2 * channels, lat_rows)
    blocks = transform(parts, legendre, load, band_count, sector_count)
    number = blocks.shape[0]
    part_basis = harmonics
    left_side = blocks.reshape(2 * number, channels * lat_rows)
    sal = lax.dot_general(
        left_side,
        part_basis,
        (((0,), (0,)), ((), ())),
        precision=PRECISE,
        preferred_element_type=jnp.float32,
    ).reshape(channels, lat_rows, lon_cols)
    sal_padded = clear_poles(with_halo(sal, (("lat", 1), ("lon", 2)), 1), band_count)
    padded = jnp.concatenate([base_padded[:channels] - sal_padded, base_padded[channels:]], axis=0)
    elevation_new, east_cell, north_cell = relax_sweep(
        padded, elevation, sea_mask, lat_start, lat_count
    )
    weights_all = sample_table()
    east_time = jnp.einsum("sc,cjl->sjl", weights_all, east_cell, precision=PRECISE)
    north_time = jnp.einsum("sc,cjl->sjl", weights_all, north_cell, precision=PRECISE)
    speeds = jnp.sqrt(east_time * east_time + north_time * north_time + SPEED_EPS * SPEED_EPS)
    friction_new = BASE_FRICTION + DRAG_COEFF * jnp.sum(speeds, axis=0) / SAMPLES
    return (elevation_new, sal, friction_new)


def solution(mesh):
    return jax.shard_map(
        on_device,
        mesh=mesh,
        in_specs=(
            P(None, "lat", "lon"),
            P("lat", "lon"),
            P("lat", "lon"),
            P("lat", "lon"),
            P(),
            P("lon", "lat", None),
            P(),
        ),
        out_specs=(P(None, "lat", "lon"), P(None, "lat", "lon"), P("lat", "lon")),
        check_vma=False,
    )
```

```python
import functools
import math

import jax
import jax.numpy as jnp
from jax import lax
from jax.experimental import pallas as pl
from jax.experimental.pallas import tpu as pltpu
from jax.sharding import PartitionSpec as P

SAMPLES = 64


FREQUENCIES = (1.0, 1.0347, 0.9582, 1.0379, 0.5018, 0.4651, 0.4986, 0.4482)
EQ_AMPS = (0.73, 0.34, 0.14, 0.09, 0.42, 0.3, 0.14, 0.06)
LAT_EDGE = 1.3614
RELAX_RATE = 0.1
BASE_FRICTION = 0.05
DRAG_COEFF = 0.5
SPEED_EPS = 0.001
STEP_TIME = 3.0
PRECISE = lax.Precision.HIGHEST


def fourier_basis(order_map, columns, lon_count):
    product = order_map[:, None] * columns[None, :] % lon_count
    angles = product.astype(jnp.float32) * (2.0 * math.pi / lon_count)
    scaling = jnp.where(
        order_map > 0, math.sqrt(2.0 / lon_count), math.sqrt(1.0 / lon_count)
    ).astype(jnp.float32)[:, None]
    harmonics = jnp.stack([jnp.cos(angles) * scaling, jnp.sin(angles) * scaling], axis=1)
    return harmonics.reshape(2 * order_map.shape[0], columns.shape[0])


def sample_table():
    sample_time = STEP_TIME * jnp.arange(SAMPLES, dtype=jnp.float32)[:, None]
    omegas = jnp.asarray(FREQUENCIES, dtype=jnp.float32)[None, :]
    phases = sample_time * omegas
    return jnp.stack([jnp.cos(phases), jnp.sin(phases)], axis=2).reshape(
        SAMPLES, 2 * len(FREQUENCIES)
    )


def sweep_kernel(
    omega_ref,
    amp_ref,
    pole_ref,
    elev_ref,
    depth_ref,
    drag_ref,
    mask_ref,
    row_halo_ref,
    col_halo_ref,
    synth_ref,
    basis_ref,
    lat_ref,
    wave_ref,
    weight_ref,
    new_ref,
    sal_ref,
    friction_ref,
    coefs,
    east_cells,
    north_cells,
):
    k = pl.program_id(0)
    channels = 2 * pl.num_programs(0)
    lat_rows, lon_cols = depth_ref.shape
    wide_rows, wide_cols = lat_rows + 8, lon_cols + 128

    def rolled(value, shift, axis):
        return pltpu.roll(value, shift % value.shape[axis], axis)

    lane = lax.broadcasted_iota(jnp.int32, (lat_rows, 128), 1)
    line = lax.broadcasted_iota(jnp.int32, (8, lon_cols), 0)

    def widened(main, field):
        right = jnp.sum(jnp.where(lane == field, col_halo_ref[0], 0.0), axis=1, keepdims=True)
        left = jnp.sum(jnp.where(lane == 64 + field, col_halo_ref[1], 0.0), axis=1, keepdims=True)
        sides = jnp.where(lane == 0, right, jnp.where(lane == 127, left, 0.0))
        below = row_halo_ref[0, pl.ds(field, 1), :]
        above = row_halo_ref[1, pl.ds(field, 1), :]
        ends = jnp.where(line == 0, below, jnp.where(line == 7, above, 0.0))
        corner = jnp.zeros((8, 128), jnp.float32)
        return jnp.concatenate(
            [
                jnp.concatenate([main, sides], axis=1),
                jnp.concatenate([ends, corner], axis=1),
            ],
            axis=0,
        )

    inverse_cos = lat_ref[:, 2:3]
    cos_face = lat_ref[:, 3:4]

    @pl.when(k == 0)
    def _():
        depth = widened(depth_ref[...] * mask_ref[...].astype(jnp.float32), channels)
        row = lax.broadcasted_iota(jnp.int32, (wide_rows, wide_cols), 0)
        depth = jnp.where(
            row == lat_rows, depth * pole_ref[0], jnp.where(row == wide_rows - 1, depth * pole_ref[1], depth)
        )
        drag = widened(drag_ref[...], channels + 1)
        for face, axis in enumerate((1, 0)):
            square = depth * rolled(depth, -1, axis)
            mean = 0.5 * (drag + rolled(drag, -1, axis))
            coefs[4 * face] = square * mean
            coefs[4 * face + 1] = square * jnp.sqrt(square)
            coefs[4 * face + 2] = mean * mean
            coefs[4 * face + 3] = square

    omega = omega_ref[k]
    kind = k // 4
    lat_shape = amp_ref[k] * jnp.where(kind == 0, lat_ref[:, 0:1], lat_ref[:, 1:2])
    surface = []
    for part in range(2):
        sal = jnp.dot(
            synth_ref[part],
            basis_ref[...],
            precision=PRECISE,
            preferred_element_type=jnp.float32,
        )
        sal_ref[part] = sal[:lat_rows, :lon_cols]
        wave = wave_ref[pl.ds(2 * kind + part, 1), :]
        surface.append(widened(elev_ref[part], 2 * k + part) - lat_shape * wave - sal)
    divergence = [None, None]
    for face, (axis, factor, cells) in enumerate(
        ((1, inverse_cos, east_cells), (0, cos_face, north_cells))
    ):
        inverse = 1.0 / (coefs[4 * face + 2] + (omega * omega) * coefs[4 * face + 3])
        real_coef = coefs[4 * face] * inverse * factor
        imag_coef = (omega * coefs[4 * face + 1]) * inverse * factor
        diff_real = rolled(surface[0], -1, axis) - surface[0]
        diff_imag = rolled(surface[1], -1, axis) - surface[1]
        fluxes = (
            imag_coef * diff_imag - real_coef * diff_real,
            -(real_coef * diff_imag + imag_coef * diff_real),
        )
        for part, flux in enumerate(fluxes):
            back = rolled(flux, 1, axis)
            change = (flux - back)[:lat_rows, :lon_cols]
            divergence[part] = change if face == 0 else divergence[part] + change
            mean = (0.5 * (flux + back))[:lat_rows, :lon_cols]
            cells[:, pl.ds(2 * k + part, 1), :] = mean.reshape(lat_rows, 1, lon_cols)
    sea_mask = mask_ref[...].astype(jnp.float32)
    inner_cos = inverse_cos[:lat_rows]
    real, imag = elev_ref[0], elev_ref[1]
    new_ref[0] = (real - RELAX_RATE * (divergence[0] * inner_cos + omega * imag)) * sea_mask
    new_ref[1] = (imag - RELAX_RATE * (divergence[1] * inner_cos - omega * real)) * sea_mask

    @pl.when(k == pl.num_programs(0) - 1)
    def _():
        weights = weight_ref[...]
        weights_top = weights.astype(jnp.bfloat16)
        weights_rest = (weights - weights_top.astype(jnp.float32)).astype(jnp.bfloat16)
        stacked = jnp.concatenate([weights_top, weights_top, weights_rest], axis=1)

        def sampled(value):
            top = value.astype(jnp.bfloat16)
            rest = (value - top.astype(jnp.float32)).astype(jnp.bfloat16)
            return jnp.dot(
                stacked,
                jnp.concatenate([top, rest, top], axis=0),
                preferred_element_type=jnp.float32,
            )

        @pl.loop(0, lat_rows)
        def _(j):
            east, north = sampled(east_cells[j]), sampled(north_cells[j])
            squares = east * east + north * north + SPEED_EPS * SPEED_EPS
            speeds = squares * lax.rsqrt(squares)
            mean = jnp.sum(speeds, axis=0, keepdims=True) * (DRAG_COEFF / SAMPLES)
            friction_ref[pl.ds(j, 1), :] = BASE_FRICTION + mean


def sweep(elevation, depth, friction, land_mask, halos, synth, basis, lat_table, waves, poles):
    channels, lat_rows, lon_cols = elevation.shape
    wide_rows, wide_cols = lat_rows + 8, lon_cols + 128
    whole = pl.BlockSpec(memory_space=pltpu.VMEM)
    scalars = pl.BlockSpec(memory_space=pltpu.SMEM)

    def pair(*shape):
        return pl.BlockSpec((2,) + shape, lambda k: (k, 0, 0))

    return pl.pallas_call(
        sweep_kernel,
        grid=(channels // 2,),
        out_shape=[
            jax.ShapeDtypeStruct(elevation.shape, jnp.float32),
            jax.ShapeDtypeStruct(elevation.shape, jnp.float32),
            jax.ShapeDtypeStruct(depth.shape, jnp.float32),
        ],
        in_specs=[scalars] * 3
        + [pair(lat_rows, lon_cols)]
        + [whole] * 5
        + [pair(wide_rows, basis.shape[0])]
        + [whole] * 4,
        out_specs=[
            pair(lat_rows, lon_cols),
            pair(lat_rows, lon_cols),
            pl.BlockSpec((lat_rows, lon_cols), lambda k: (0, 0)),
        ],
        scratch_shapes=[
            pltpu.VMEM((8, wide_rows, wide_cols), jnp.float32),
            pltpu.VMEM((lat_rows, channels, lon_cols), jnp.float32),
            pltpu.VMEM((lat_rows, channels, lon_cols), jnp.float32),
        ],
        compiler_params=pltpu.CompilerParams(
            dimension_semantics=("arbitrary",), vmem_limit_bytes=40 * 1024 * 1024
        ),
    )(
        jnp.asarray(FREQUENCIES, dtype=jnp.float32),
        jnp.asarray(EQ_AMPS, dtype=jnp.float32),
        poles,
        elevation,
        depth,
        friction,
        land_mask,
        *halos,
        synth,
        basis,
        lat_table,
        waves,
        sample_table(),
    )


GROUPS = 4
MESH = pl.DeviceIdType.MESH


def transform_kernel(
    lat_size,
    lon_size,
    groups,
    part_ref,
    leg_ref,
    load_ref,
    leg_edges_ref,
    row_edges_ref,
    col_edges_ref,
    out_ref,
    row_halo_ref,
    col_halo_ref,
    sector_parts,
    fourier,
    leg_halo,
    synth,
    synth_edges,
    acc,
    first_recv,
    rs_send,
    rs_recv,
    gathered,
    lon_send,
    lon_recv,
    out_send,
    out_recv,
    red_send,
    red_recv,
    gat_send,
    gat_recv,
    halo_send,
    halo_recv,
):
    lat_me = lax.axis_index("lat")
    lon_me = lax.axis_index("lon")
    levels = lat_size.bit_length() - 1
    slots, lat_rows, degrees = leg_ref.shape
    quantities = part_ref.shape[2]
    rows = slots * quantities
    width = degrees // groups
    bits = [(lat_me // 2**k) % 2 for k in range(levels)]
    partners = [lat_me + (1 - 2 * bits[k]) * 2**k for k in range(levels)]
    others = [lax.rem(lon_me + d, lon_size) for d in range(1, lon_size)]
    kept, sent = [0], []
    for k in range(levels):
        half = rows >> (k + 1)
        sent.append(pl.multiple_of(kept[k] + (1 - bits[k]) * half, half))
        kept.append(pl.multiple_of(kept[k] + bits[k] * half, half))

    barrier = pltpu.get_barrier_semaphore()
    for k in range(levels):
        pl.semaphore_signal(
            barrier, inc=1, device_id=(partners[k], lon_me), device_id_type=MESH
        )
    for other in others:
        pl.semaphore_signal(barrier, inc=1, device_id=(lat_me, other), device_id_type=MESH)
    above, below = lax.rem(lat_me + lat_size - 1, lat_size), lax.rem(lat_me + 1, lat_size)
    left, right = lax.rem(lon_me + lon_size - 1, lon_size), lax.rem(lon_me + 1, lon_size)
    for near in (above, below):
        pl.semaphore_signal(barrier, inc=1, device_id=(near, lon_me), device_id_type=MESH)
    pl.semaphore_wait(barrier, levels + lon_size + 1)

    pending = []

    def send(source, target, send_sem, recv_sem, device):
        copy = pltpu.make_async_remote_copy(
            src_ref=source,
            dst_ref=target,
            send_sem=send_sem,
            recv_sem=recv_sem,
            device_id=device,
            device_id_type=MESH,
        )
        copy.start()
        pending.append(copy)
        return copy

    copies = [
        send(
            part_ref.at[other],
            sector_parts.at[d],
            lon_send.at[d],
            lon_recv.at[d],
            (lat_me, other),
        )
        for d, other in enumerate(others)
    ]
    halos = [
        send(source, target, halo_send.at[n], halo_recv.at[n], device)
        for n, (source, target, device) in enumerate(
            (
                (leg_edges_ref.at[0], leg_halo.at[pl.ds(0, slots)], (above, lon_me)),
                (leg_edges_ref.at[1], leg_halo.at[pl.ds(slots, slots)], (below, lon_me)),
                (row_edges_ref.at[0], row_halo_ref.at[0], (above, lon_me)),
                (row_edges_ref.at[1], row_halo_ref.at[1], (below, lon_me)),
                (col_edges_ref, col_halo_ref.at[0], (lat_me, left)),
                (col_edges_ref, col_halo_ref.at[1], (lat_me, right)),
            )
        )
    ]
    for copy in copies:
        copy.wait_recv()
    total = part_ref[lon_me]
    for d in range(lon_size - 1):
        total = total + sector_parts[d]
    fourier[...] = total.astype(jnp.bfloat16)

    reducing = {}
    gathering = {}

    def analyse(g):
        @pl.loop(0, slots)
        def _(s):
            acc[g, pl.ds(pl.multiple_of(s * quantities, quantities), quantities), :] = jnp.dot(
                fourier[s],
                leg_ref[s, :, g * width : (g + 1) * width],
                preferred_element_type=jnp.float32,
            )

        reducing[g] = send(
            acc.at[g, pl.ds(sent[0], rows // 2), :],
            first_recv.at[g],
            red_send.at[g, 0],
            red_recv.at[g, 0],
            (partners[0], lon_me),
        )

    def offset_of(k):
        return rows // 2 - (rows >> k)

    def reduce(g, k):
        reducing[g].wait_recv()
        size = rows >> (k + 1)

        def arrived(start, count):
            if k == 0:
                return first_recv[g, pl.ds(start, count), :]
            return rs_recv[g, pl.ds(offset_of(k) + start, count), :].astype(jnp.float32)

        if k < levels - 1:
            half = size // 2
            away = pl.multiple_of((1 - bits[k + 1]) * half, half)
            home = pl.multiple_of(bits[k + 1] * half, half)
            place = pl.ds(offset_of(k + 1), half)
            rs_send[g, place, :] = (
                acc[g, pl.ds(sent[k + 1], half), :] + arrived(away, half)
            ).astype(jnp.bfloat16)
            reducing[g] = send(
                rs_send.at[g, place, :],
                rs_recv.at[g, place, :],
                red_send.at[g, k + 1],
                red_recv.at[g, k + 1],
                (partners[k + 1], lon_me),
            )
            acc[g, pl.ds(kept[k + 1 + 1], half), :] = acc[
                g, pl.ds(kept[k + 1 + 1], half), :
            ] + arrived(home, half)
        else:
            mine = pl.ds(kept[levels], size)
            scale = load_ref[:, g * width : (g + 1) * width]
            gathered[g, mine, :] = ((acc[g, mine, :] + arrived(0, size)) * scale).astype(
                jnp.bfloat16
            )
            spread(g, levels - 1)

    def spread(g, k):
        held = pl.ds(kept[k + 1], rows >> (k + 1))
        gathering[g] = send(
            gathered.at[g, held, :],
            gathered.at[g, held, :],
            gat_send.at[g, k],
            gat_recv.at[g, k],
            (partners[k], lon_me),
        )

    def synthesise(g):
        if g == 0:
            for copy in halos[:2]:
                copy.wait_recv()
        at_edges = lax.dot_general(
            gathered[g],
            leg_halo[:, g * width : (g + 1) * width],
            (((1,), (1,)), ((), ())),
            preferred_element_type=jnp.float32,
        )
        if g == 0:
            synth_edges[...] = at_edges
        else:
            synth_edges[...] = synth_edges[...] + at_edges

        @pl.loop(0, slots)
        def _(s):
            part = lax.dot_general(
                gathered[g, pl.ds(pl.multiple_of(s * quantities, quantities), quantities), :],
                leg_ref[s, :, g * width : (g + 1) * width],
                (((1,), (1,)), ((), ())),
                preferred_element_type=jnp.float32,
            )
            if g == 0:
                synth[s] = part
            else:
                synth[s] = synth[s] + part

    def gather(g, k):
        gathering[g].wait_recv()
        if k > 0:
            spread(g, k - 1)
        else:
            synthesise(g)

    for wave in range(groups + 2 * levels):
        for g in range(groups):
            stage = wave - g
            if stage == 0:
                analyse(g)
            elif 1 <= stage <= levels:
                reduce(g, stage - 1)
            elif levels < stage <= 2 * levels:
                gather(g, 2 * levels - stage)

    lanes = lax.broadcasted_iota(jnp.int32, (quantities, 2 * slots), 1)
    places = lax.broadcasted_iota(jnp.int32, (quantities, out_ref.shape[2] - lat_rows), 1)

    @pl.loop(0, slots)
    def _(s):
        edges = synth_edges[pl.ds(pl.multiple_of(s * quantities, quantities), quantities), :]
        after = jnp.sum(jnp.where(lanes == s, edges, 0.0), axis=1, keepdims=True)
        before = jnp.sum(jnp.where(lanes == slots + s, edges, 0.0), axis=1, keepdims=True)
        out_ref[lon_me * slots + s, :, :lat_rows] = synth[s]
        out_ref[lon_me * slots + s, :, lat_rows:] = jnp.where(
            places == 0, after, jnp.where(places == 7, before, 0.0)
        )

    block = out_ref.at[pl.ds(lon_me * slots, slots)]
    copies = [
        send(block, block, out_send.at[d], out_recv.at[d], (lat_me, other))
        for d, other in enumerate(others)
    ]
    for copy in copies + halos[2:]:
        copy.wait_recv()
    for copy in pending:
        copy.wait_send()


def transform(parts, legendre, load, edges, lat_size, lon_size):
    slots, lat_rows, degrees = legendre.shape
    quantities = parts.shape[2]
    rows = slots * quantities
    groups = GROUPS
    width = degrees // groups
    levels = lat_size.bit_length() - 1
    vmem = pl.BlockSpec(memory_space=pltpu.VMEM)
    dma = pltpu.SemaphoreType.DMA
    flops = 4 * rows * lat_rows * degrees
    return pl.pallas_call(
        functools.partial(transform_kernel, lat_size, lon_size, groups),
        out_shape=[
            jax.ShapeDtypeStruct((lon_size * slots, quantities, 128), jnp.float32),
            jax.ShapeDtypeStruct(edges[1].shape, jnp.float32),
            jax.ShapeDtypeStruct((2,) + edges[2].shape, jnp.float32),
        ],
        in_specs=[vmem] * 6,
        out_specs=[vmem] * 3,
        scratch_shapes=[
            pltpu.VMEM((lon_size - 1, slots, quantities, lat_rows), jnp.float32),
            pltpu.VMEM((slots, quantities, lat_rows), jnp.bfloat16),
            pltpu.VMEM((2 * slots, degrees), jnp.bfloat16),
            pltpu.VMEM((slots, quantities, lat_rows), jnp.float32),
            pltpu.VMEM((rows, 2 * slots), jnp.float32),
            pltpu.VMEM((groups, rows, width), jnp.float32),
            pltpu.VMEM((groups, rows // 2, width), jnp.float32),
            pltpu.VMEM((groups, rows // 2, width), jnp.bfloat16),
            pltpu.VMEM((groups, rows // 2, width), jnp.bfloat16),
            pltpu.VMEM((groups, rows, width), jnp.bfloat16),
            dma((lon_size - 1,)),
            dma((lon_size - 1,)),
            dma((lon_size - 1,)),
            dma((lon_size - 1,)),
            dma((groups, levels)),
            dma((groups, levels)),
            dma((groups, levels)),
            dma((groups, levels)),
            dma((6,)),
            dma((6,)),
        ],
        compiler_params=pltpu.CompilerParams(
            collective_id=0, has_side_effects=True, vmem_limit_bytes=40 * 1024 * 1024
        ),
        cost_estimate=pl.CostEstimate(
            flops=flops, bytes_accessed=2 * slots * lat_rows * degrees, transcendentals=0
        ),
    )(parts, legendre, load[None, :], *edges)


def on_device(elevation, depth, friction, land_mask, order_map, legendre, load):
    channels, lat_rows, lon_cols = elevation.shape
    slot_count = legendre.shape[0]
    band_count = lax.axis_size("lat")
    sector_count = lax.axis_size("lon")
    lat_count = lat_rows * band_count
    lon_count = lon_cols * sector_count
    band = lax.axis_index("lat")
    lat_start = band * lat_rows
    col_start = lax.axis_index("lon") * lon_cols
    sea_mask = land_mask.astype(jnp.float32)
    sea_depth = depth * sea_mask

    steps = jnp.arange(lon_cols + 128, dtype=jnp.int32)
    steps = jnp.where(steps == lon_cols + 127, -1, steps)
    columns = (col_start + steps + lon_count) % lon_count
    basis = fourier_basis(order_map, columns, lon_count)
    longitude = columns.astype(jnp.float32) * (2.0 * math.pi / lon_count)
    waves = jnp.stack(
        [jnp.cos(2.0 * longitude), jnp.sin(2.0 * longitude), jnp.cos(longitude), jnp.sin(longitude)]
    )
    lines = jnp.arange(lat_rows + 8, dtype=jnp.int32)
    lines = lat_start + jnp.where(lines == lat_rows + 7, -1, lines)
    lat_step = 2.0 * LAT_EDGE / lat_count
    latitude = -LAT_EDGE + (lines.astype(jnp.float32) + 0.5) * lat_step
    face_latitude = -LAT_EDGE + (lines.astype(jnp.float32) + 1.0) * lat_step
    lat_table = jnp.stack(
        [
            jnp.cos(latitude) ** 2,
            jnp.sin(2.0 * latitude),
            1.0 / jnp.cos(latitude),
            jnp.cos(face_latitude),
        ],
        axis=1,
    )
    poles = jnp.stack([band < band_count - 1, band > 0]).astype(jnp.float32)

    leg_edges = jnp.stack([legendre[:, 0], legendre[:, -1]])
    row_edges = jnp.stack(
        [
            jnp.concatenate([elevation[:, j], sea_depth[None, j], friction[None, j]], axis=0)
            for j in (0, lat_rows - 1)
        ]
    )
    col_edges = jnp.concatenate(
        [
            jnp.pad(
                jnp.concatenate([elevation[:, :, i], sea_depth[None, :, i], friction[None, :, i]]),
                ((0, 62 - channels), (0, 0)),
            )
            for i in (0, lon_cols - 1)
        ]
    ).T

    flat_field = (elevation * sea_mask).reshape(channels * lat_rows, lon_cols)
    product = lax.dot_general(
        basis[:, :lon_cols],
        flat_field,
        (((1,), (1,)), ((), ())),
        precision=PRECISE,
        preferred_element_type=jnp.float32,
    )
    parts = product.reshape(sector_count, slot_count, 2 * channels, lat_rows)
    blocks, row_halo, col_halo = transform(
        parts, legendre, load, (leg_edges, row_edges, col_edges), band_count, sector_count
    )
    synth = blocks[:, :, : lat_rows + 8].reshape(-1, 2, channels, lat_rows + 8)
    synth = synth.transpose(2, 3, 0, 1).reshape(channels, lat_rows + 8, basis.shape[0])
    return tuple(
        sweep(
            elevation,
            depth,
            friction,
            land_mask,
            (row_halo, col_halo),
            synth,
            basis,
            lat_table,
            waves,
            poles,
        )
    )


def solution(mesh):
    return jax.shard_map(
        on_device,
        mesh=mesh,
        in_specs=(
            P(None, "lat", "lon"),
            P("lat", "lon"),
            P("lat", "lon"),
            P("lat", "lon"),
            P(),
            P("lon", "lat", None),
            P(),
        ),
        out_specs=(P(None, "lat", "lon"), P(None, "lat", "lon"), P("lat", "lon")),
        check_vma=False,
    )
```

```python
import functools
import math

import jax
import jax.numpy as jnp
from jax import lax
from jax.experimental import pallas as pl
from jax.experimental.pallas import tpu as pltpu
from jax.sharding import PartitionSpec as P

SAMPLES = 64


FREQUENCIES = (1.0, 1.0347, 0.9582, 1.0379, 0.5018, 0.4651, 0.4986, 0.4482)
EQ_AMPS = (0.73, 0.34, 0.14, 0.09, 0.42, 0.3, 0.14, 0.06)
LAT_EDGE = 1.3614
RELAX_RATE = 0.1
BASE_FRICTION = 0.05
DRAG_COEFF = 0.5
SPEED_EPS = 0.001
STEP_TIME = 3.0
PRECISE = lax.Precision.HIGHEST


def fourier_basis(order_map, columns, lon_count):
    product = order_map[:, None] * columns[None, :] % lon_count
    angles = product.astype(jnp.float32) * (2.0 * math.pi / lon_count)
    scaling = jnp.where(
        order_map > 0, math.sqrt(2.0 / lon_count), math.sqrt(1.0 / lon_count)
    ).astype(jnp.float32)[:, None]
    harmonics = jnp.stack([jnp.cos(angles) * scaling, jnp.sin(angles) * scaling], axis=1)
    return harmonics.reshape(2 * order_map.shape[0], columns.shape[0])


def sample_table():
    sample_time = STEP_TIME * jnp.arange(SAMPLES, dtype=jnp.float32)[:, None]
    omegas = jnp.asarray(FREQUENCIES, dtype=jnp.float32)[None, :]
    phases = sample_time * omegas
    return jnp.stack([jnp.cos(phases), jnp.sin(phases)], axis=2).reshape(
        SAMPLES, 2 * len(FREQUENCIES)
    )


def sweep_kernel(
    omega_ref,
    amp_ref,
    pole_ref,
    elev_ref,
    depth_ref,
    drag_ref,
    mask_ref,
    row_halo_ref,
    col_halo_ref,
    synth_ref,
    basis_ref,
    lat_ref,
    wave_ref,
    weight_ref,
    new_ref,
    sal_ref,
    friction_ref,
    coefs,
    east_cells,
    north_cells,
):
    k = pl.program_id(0)
    channels = 2 * pl.num_programs(0)
    lat_rows, lon_cols = depth_ref.shape
    wide_rows, wide_cols = lat_rows + 8, lon_cols + 128

    def rolled(value, shift, axis):
        return pltpu.roll(value, shift % value.shape[axis], axis)

    lane = lax.broadcasted_iota(jnp.int32, (lat_rows, 128), 1)
    line = lax.broadcasted_iota(jnp.int32, (8, lon_cols), 0)

    def widened(main, field):
        right = jnp.sum(jnp.where(lane == field, col_halo_ref[0], 0.0), axis=1, keepdims=True)
        left = jnp.sum(jnp.where(lane == 64 + field, col_halo_ref[1], 0.0), axis=1, keepdims=True)
        sides = jnp.where(lane == 0, right, jnp.where(lane == 127, left, 0.0))
        below = row_halo_ref[0, pl.ds(field, 1), :]
        above = row_halo_ref[1, pl.ds(field, 1), :]
        ends = jnp.where(line == 0, below, jnp.where(line == 7, above, 0.0))
        corner = jnp.zeros((8, 128), jnp.float32)
        return jnp.concatenate(
            [
                jnp.concatenate([main, sides], axis=1),
                jnp.concatenate([ends, corner], axis=1),
            ],
            axis=0,
        )

    inverse_cos = lat_ref[:, 2:3]
    cos_face = lat_ref[:, 3:4]

    @pl.when(k == 0)
    def _():
        depth = widened(depth_ref[...] * mask_ref[...].astype(jnp.float32), channels)
        row = lax.broadcasted_iota(jnp.int32, (wide_rows, wide_cols), 0)
        depth = jnp.where(
            row == lat_rows, depth * pole_ref[0], jnp.where(row == wide_rows - 1, depth * pole_ref[1], depth)
        )
        drag = widened(drag_ref[...], channels + 1)
        for face, axis in enumerate((1, 0)):
            square = depth * rolled(depth, -1, axis)
            mean = 0.5 * (drag + rolled(drag, -1, axis))
            coefs[4 * face] = square * mean
            coefs[4 * face + 1] = square * jnp.sqrt(square)
            coefs[4 * face + 2] = mean * mean
            coefs[4 * face + 3] = square

    omega = omega_ref[k]
    kind = k // 4
    lat_shape = amp_ref[k] * jnp.where(kind == 0, lat_ref[:, 0:1], lat_ref[:, 1:2])
    surface = []
    for part in range(2):
        sal = jnp.dot(
            synth_ref[part],
            basis_ref[...],
            precision=PRECISE,
            preferred_element_type=jnp.float32,
        )
        sal_ref[part] = sal[:lat_rows, :lon_cols]
        wave = wave_ref[pl.ds(2 * kind + part, 1), :]
        surface.append(widened(elev_ref[part], 2 * k + part) - lat_shape * wave - sal)
    divergence = [None, None]
    for face, (axis, factor, cells) in enumerate(
        ((1, inverse_cos, east_cells), (0, cos_face, north_cells))
    ):
        inverse = 1.0 / (coefs[4 * face + 2] + (omega * omega) * coefs[4 * face + 3])
        real_coef = coefs[4 * face] * inverse * factor
        imag_coef = (omega * coefs[4 * face + 1]) * inverse * factor
        diff_real = rolled(surface[0], -1, axis) - surface[0]
        diff_imag = rolled(surface[1], -1, axis) - surface[1]
        fluxes = (
            imag_coef * diff_imag - real_coef * diff_real,
            -(real_coef * diff_imag + imag_coef * diff_real),
        )
        for part, flux in enumerate(fluxes):
            back = rolled(flux, 1, axis)
            change = (flux - back)[:lat_rows, :lon_cols]
            divergence[part] = change if face == 0 else divergence[part] + change
            mean = (0.5 * (flux + back))[:lat_rows, :lon_cols]
            cells[:, pl.ds(2 * k + part, 1), :] = mean.reshape(lat_rows, 1, lon_cols)
    sea_mask = mask_ref[...].astype(jnp.float32)
    inner_cos = inverse_cos[:lat_rows]
    real, imag = elev_ref[0], elev_ref[1]
    new_ref[0] = (real - RELAX_RATE * (divergence[0] * inner_cos + omega * imag)) * sea_mask
    new_ref[1] = (imag - RELAX_RATE * (divergence[1] * inner_cos - omega * real)) * sea_mask

    @pl.when(k == pl.num_programs(0) - 1)
    def _():
        weights = weight_ref[...]
        weights_top = weights.astype(jnp.bfloat16)
        weights_rest = (weights - weights_top.astype(jnp.float32)).astype(jnp.bfloat16)
        stacked = jnp.concatenate([weights_top, weights_top, weights_rest], axis=1)

        def sampled(value):
            top = value.astype(jnp.bfloat16)
            rest = (value - top.astype(jnp.float32)).astype(jnp.bfloat16)
            return jnp.dot(
                stacked,
                jnp.concatenate([top, rest, top], axis=0),
                preferred_element_type=jnp.float32,
            )

        @pl.loop(0, lat_rows, unroll=UNROLL)
        def _(j):
            east, north = sampled(east_cells[j]), sampled(north_cells[j])
            squares = east * east + north * north + SPEED_EPS * SPEED_EPS
            speeds = squares * lax.rsqrt(squares)
            mean = jnp.sum(speeds, axis=0, keepdims=True) * (DRAG_COEFF / SAMPLES)
            friction_ref[pl.ds(j, 1), :] = BASE_FRICTION + mean


def sweep(elevation, depth, friction, land_mask, halos, synth, basis, lat_table, waves, poles):
    channels, lat_rows, lon_cols = elevation.shape
    wide_rows, wide_cols = lat_rows + 8, lon_cols + 128
    whole = pl.BlockSpec(memory_space=pltpu.VMEM)
    scalars = pl.BlockSpec(memory_space=pltpu.SMEM)

    def fixed(value):
        return pl.BlockSpec(value.shape, lambda k: (0,) * value.ndim)

    def pair(*shape):
        return pl.BlockSpec((2,) + shape, lambda k: (k, 0, 0))

    return pl.pallas_call(
        sweep_kernel,
        grid=(channels // 2,),
        out_shape=[
            jax.ShapeDtypeStruct(elevation.shape, jnp.float32),
            jax.ShapeDtypeStruct(elevation.shape, jnp.float32),
            jax.ShapeDtypeStruct(depth.shape, jnp.float32),
        ],
        in_specs=[scalars] * 3
        + [pair(lat_rows, lon_cols)]
        + [fixed(value) for value in (depth, friction, land_mask) + halos]
        + [pair(wide_rows, basis.shape[0])]
        + [fixed(basis), fixed(lat_table), fixed(waves), whole],
        out_specs=[
            pair(lat_rows, lon_cols),
            pair(lat_rows, lon_cols),
            pl.BlockSpec((lat_rows, lon_cols), lambda k: (0, 0)),
        ],
        scratch_shapes=[
            pltpu.VMEM((8, wide_rows, wide_cols), jnp.float32),
            pltpu.VMEM((lat_rows, channels, lon_cols), jnp.float32),
            pltpu.VMEM((lat_rows, channels, lon_cols), jnp.float32),
        ],
        compiler_params=pltpu.CompilerParams(
            dimension_semantics=("arbitrary",), vmem_limit_bytes=40 * 1024 * 1024
        ),
    )(
        jnp.asarray(FREQUENCIES, dtype=jnp.float32),
        jnp.asarray(EQ_AMPS, dtype=jnp.float32),
        poles,
        elevation,
        depth,
        friction,
        land_mask,
        *halos,
        synth,
        basis,
        lat_table,
        waves,
        sample_table(),
    )


GROUPS = 4
UNROLL = 16
MESH = pl.DeviceIdType.MESH


def lat_factors(lat_size):
    return (2, lat_size // 8, 4)


def transform_kernel(
    factors,
    lon_size,
    groups,
    part_ref,
    leg_hbm,
    load_ref,
    leg_edges_ref,
    elev_hbm,
    depth_hbm,
    drag_hbm,
    mask_hbm,
    out_ref,
    row_halo_ref,
    col_halo_ref,
    leg_ref,
    row_strips,
    col_strips,
    row_masks,
    col_masks,
    row_edges,
    col_edges,
    packed_out,
    packed_in,
    fourier,
    leg_halo,
    synth,
    synth_edges,
    packed_synth,
    packed_edges,
    acc,
    first_recv,
    rs_send,
    rs_recv,
    gathered,
    leg_sem,
    strip_sem,
    lon_send,
    lon_recv,
    out_send,
    out_recv,
    red_send,
    red_recv,
    gat_send,
    gat_recv,
    halo_send,
    halo_recv,
):
    lat_me = lax.axis_index("lat")
    lon_me = lax.axis_index("lon")
    lat_size = math.prod(factors)
    phases = len(factors)
    slots, lat_rows, degrees = leg_ref.shape
    quantities = part_ref.shape[2]
    channels = elev_hbm.shape[0]
    lon_cols = elev_hbm.shape[2]
    rows = slots * quantities
    width = degrees // groups
    pairs = slots // 2

    loads = [pltpu.make_async_copy(leg_hbm, leg_ref, leg_sem.at[0])]
    for side in range(2):
        top, first = side * (lat_rows - 8), side * (lon_cols - 128)
        for n, (field, row_to, col_to) in enumerate(
            (
                (elev_hbm, row_strips.at[side, :channels], col_strips.at[side, :channels]),
                (depth_hbm, row_strips.at[side, channels], col_strips.at[side, channels]),
                (drag_hbm, row_strips.at[side, channels + 1], col_strips.at[side, channels + 1]),
                (mask_hbm, row_masks.at[side], col_masks.at[side]),
            )
        ):
            lead = (slice(None),) if n == 0 else ()
            row_from = field.at[lead + (pl.ds(top, 8), slice(None))]
            col_from = field.at[lead + (slice(None), pl.ds(first, 128))]
            loads.append(pltpu.make_async_copy(row_from, row_to, strip_sem.at[side, n]))
            loads.append(pltpu.make_async_copy(col_from, col_to, strip_sem.at[side, 4 + n]))
    for copy in loads[1:] + loads[:1]:
        copy.start()

    digits, peers, kept, sizes = [], [], [0], [rows]
    stride = 1
    for factor in factors:
        digit = (lat_me // stride) % factor
        around = [(digit + d) % factor for d in range(1, factor)]
        digits.append(digit)
        peers.append([(other, lat_me + (other - digit) * stride) for other in around])
        sizes.append(sizes[-1] // factor)
        kept.append(pl.multiple_of(kept[-1] + digit * sizes[-1], sizes[-1]))
        stride *= factor
    others = [lax.rem(lon_me + d, lon_size) for d in range(1, lon_size)]
    above, below = lax.rem(lat_me + lat_size - 1, lat_size), lax.rem(lat_me + 1, lat_size)
    left, right = lax.rem(lon_me + lon_size - 1, lon_size), lax.rem(lon_me + 1, lon_size)

    barrier = pltpu.get_barrier_semaphore()
    greeted = [(other, lon_me) for phase in peers for _, other in phase]
    greeted += [(above, lon_me), (below, lon_me)] + [(lat_me, other) for other in others]
    for device in greeted:
        pl.semaphore_signal(barrier, inc=1, device_id=device, device_id_type=MESH)
    for d, other in enumerate(others):
        packed_out[d, :, :, :lat_rows] = part_ref[other, :pairs]
        packed_out[d, :, :, lat_rows:] = part_ref[other, pairs:]
    pl.semaphore_wait(barrier, len(greeted))

    pending = []

    def send(source, target, send_sem, recv_sem, device):
        copy = pltpu.make_async_remote_copy(
            src_ref=source,
            dst_ref=target,
            send_sem=send_sem,
            recv_sem=recv_sem,
            device_id=device,
            device_id_type=MESH,
        )
        copy.start()
        pending.append(copy)
        return copy

    copies = [
        send(packed_out.at[d], packed_in.at[d], lon_send.at[d], lon_recv.at[d], (lat_me, other))
        for d, other in enumerate(others)
    ]

    for copy in loads[1:]:
        copy.wait()
    lane = lax.broadcasted_iota(jnp.int32, (lat_rows, 128), 1)
    edge_cols = jnp.zeros((lat_rows, 128), jnp.float32)
    for side in range(2):
        row, col = 7 * side, 127 * side
        for field in range(channels + 2):
            line = row_strips[side, field, row : row + 1, :]
            column = col_strips[side, field, :, col : col + 1]
            if field == channels:
                line = line * row_masks[side, row : row + 1, :].astype(jnp.float32)
                column = column * col_masks[side, :, col : col + 1].astype(jnp.float32)
            row_edges[side, field : field + 1, :] = line
            edge_cols = jnp.where(lane == 64 * side + field, column, edge_cols)
    col_edges[...] = edge_cols
    halos = [
        send(source, target, halo_send.at[n], halo_recv.at[n], device)
        for n, (source, target, device) in enumerate(
            (
                (leg_edges_ref.at[0], leg_halo.at[pl.ds(0, slots)], (above, lon_me)),
                (leg_edges_ref.at[1], leg_halo.at[pl.ds(slots, slots)], (below, lon_me)),
                (row_edges.at[0], row_halo_ref.at[0], (above, lon_me)),
                (row_edges.at[1], row_halo_ref.at[1], (below, lon_me)),
                (col_edges, col_halo_ref.at[0], (lat_me, left)),
                (col_edges, col_halo_ref.at[1], (lat_me, right)),
            )
        )
    ]
    for copy in copies:
        copy.wait_recv()
    for half in range(2):
        total = part_ref[lon_me, half * pairs : (half + 1) * pairs]
        for d in range(lon_size - 1):
            total = total + packed_in[d, :, :, half * lat_rows : (half + 1) * lat_rows]
        fourier[half * pairs : (half + 1) * pairs] = total.astype(jnp.bfloat16)
    loads[0].wait()

    reducing = {}
    gathering = {}
    offsets = [0, 0]
    for p in range(1, phases):
        offsets.append(offsets[-1] + (factors[p] - 1) * sizes[p + 1])

    def analyse(g):
        @pl.loop(0, slots, unroll=UNROLL)
        def _(s):
            acc[g, pl.ds(pl.multiple_of(s * quantities, quantities), quantities), :] = jnp.dot(
                fourier[s],
                leg_ref[s, :, g * width : (g + 1) * width],
                preferred_element_type=jnp.float32,
            )

        away = pl.multiple_of(peers[0][0][0] * sizes[1], sizes[1])
        reducing[g] = [
            send(
                acc.at[g, pl.ds(away, sizes[1]), :],
                first_recv.at[g],
                red_send.at[g, 0, 0],
                red_recv.at[g, 0, 0],
                (peers[0][0][1], lon_me),
            )
        ]

    def reduce(g, p):
        for copy in reducing[g]:
            copy.wait_recv()
        size = sizes[p + 1]

        def value(start, count):
            total = acc[g, pl.ds(pl.multiple_of(kept[p + 1] + start, count), count), :]
            if p == 0:
                return total + first_recv[g, pl.ds(start, count), :]
            for d in range(factors[p] - 1):
                place = pl.multiple_of(offsets[p] + d * size + start, 16)
                total = total + rs_recv[g, pl.ds(place, count), :].astype(jnp.float32)
            return total

        if p < phases - 1:
            sub = sizes[p + 2]
            reducing[g] = []
            for d, (digit, device) in enumerate(peers[p + 1]):
                place = pl.ds(offsets[p + 1] + d * sub, sub)
                rs_send[g, place, :] = value(pl.multiple_of(digit * sub, sub), sub).astype(
                    jnp.bfloat16
                )
                reducing[g].append(
                    send(
                        rs_send.at[g, place, :],
                        rs_recv.at[g, place, :],
                        red_send.at[g, p + 1, d],
                        red_recv.at[g, p + 1, d],
                        (device, lon_me),
                    )
                )
            acc[g, pl.ds(kept[p + 2], sub), :] = value(
                pl.multiple_of(digits[p + 1] * sub, sub), sub
            )
        else:
            scale = load_ref[:, g * width : (g + 1) * width]
            gathered[g, pl.ds(kept[phases], size), :] = (value(0, size) * scale).astype(
                jnp.bfloat16
            )
            spread(g, phases - 1)

    def spread(g, p):
        held = pl.ds(kept[p + 1], sizes[p + 1])
        gathering[g] = [
            send(
                gathered.at[g, held, :],
                gathered.at[g, held, :],
                gat_send.at[g, p, d],
                gat_recv.at[g, p, d],
                (device, lon_me),
            )
            for d, (_, device) in enumerate(peers[p])
        ]

    def synthesise(g):
        if g == 0:
            for copy in halos[:2]:
                copy.wait_recv()
        at_edges = lax.dot_general(
            gathered[g],
            leg_halo[:, g * width : (g + 1) * width],
            (((1,), (1,)), ((), ())),
            preferred_element_type=jnp.float32,
        )
        if g == 0:
            synth_edges[...] = at_edges
        else:
            synth_edges[...] = synth_edges[...] + at_edges

        @pl.loop(0, slots, unroll=UNROLL)
        def _(s):
            part = lax.dot_general(
                gathered[g, pl.ds(pl.multiple_of(s * quantities, quantities), quantities), :],
                leg_ref[s, :, g * width : (g + 1) * width],
                (((1,), (1,)), ((), ())),
                preferred_element_type=jnp.float32,
            )
            if g == 0:
                synth[s] = part
            else:
                synth[s] = synth[s] + part

    def gather(g, p):
        for copy in gathering[g]:
            copy.wait_recv()
        if p > 0:
            spread(g, p - 1)
        else:
            synthesise(g)

    for wave in range(groups + 2 * phases):
        for g in range(groups):
            stage = wave - g
            if stage == 0:
                analyse(g)
            elif 1 <= stage <= phases:
                reduce(g, stage - 1)
            elif phases < stage <= 2 * phases:
                gather(g, 2 * phases - stage)

    packed_synth[lon_me, :, :, :lat_rows] = synth[:pairs]
    packed_synth[lon_me, :, :, lat_rows:] = synth[pairs:]
    edge_lane = lax.broadcasted_iota(jnp.int32, (quantities, 2 * slots), 1) % slots
    edges = jnp.zeros((quantities, 2 * slots), jnp.float32)
    for s in range(slots):
        edges = jnp.where(
            edge_lane == s, synth_edges[s * quantities : (s + 1) * quantities, :], edges
        )
    packed_edges[lon_me] = edges
    copies = []
    for d, other in enumerate(others):
        for n, array in enumerate((packed_synth, packed_edges)):
            copies.append(
                send(
                    array.at[lon_me],
                    array.at[lon_me],
                    out_send.at[d, n],
                    out_recv.at[d, n],
                    (lat_me, other),
                )
            )
    places = lax.broadcasted_iota(jnp.int32, (quantities, out_ref.shape[2] - lat_rows), 1)

    def unpack(block):
        both = packed_edges[block]
        for s in range(slots):
            slot = block * slots + s
            half = s // pairs
            out_ref[slot, :, :lat_rows] = packed_synth[
                block, s % pairs, :, half * lat_rows : (half + 1) * lat_rows
            ]
            out_ref[slot, :, lat_rows:] = jnp.where(
                places == 0,
                both[:, s : s + 1],
                jnp.where(places == 7, both[:, slots + s : slots + s + 1], 0.0),
            )

    unpack(lon_me)
    for copy in copies + halos[2:]:
        copy.wait_recv()
    for other in others:
        unpack(other)
    for copy in pending:
        copy.wait_send()


def transform(parts, legendre, load, leg_edges, fields, lat_size, lon_size):
    slots, lat_rows, degrees = legendre.shape
    quantities = parts.shape[2]
    channels, _, lon_cols = fields[0].shape
    rows = slots * quantities
    groups = GROUPS
    width = degrees // groups
    factors = lat_factors(lat_size)
    staged, size = 0, rows // factors[0]
    for factor in factors[1:]:
        size //= factor
        staged += (factor - 1) * size
    vmem = pl.BlockSpec(memory_space=pltpu.VMEM)
    anywhere = pl.BlockSpec(memory_space=pl.ANY)
    dma = pltpu.SemaphoreType.DMA
    most = (groups, len(factors), max(factors) - 1)
    f32, bf16 = jnp.float32, jnp.bfloat16
    return pl.pallas_call(
        functools.partial(transform_kernel, factors, lon_size, groups),
        out_shape=[
            jax.ShapeDtypeStruct((lon_size * slots, quantities, 128), f32),
            jax.ShapeDtypeStruct((2, channels + 2, lon_cols), f32),
            jax.ShapeDtypeStruct((2, lat_rows, 128), f32),
        ],
        in_specs=[vmem, anywhere, vmem, vmem] + [anywhere] * 4,
        out_specs=[vmem] * 3,
        scratch_shapes=[
            pltpu.VMEM(legendre.shape, bf16),
            pltpu.VMEM((2, channels + 2, 8, lon_cols), f32),
            pltpu.VMEM((2, channels + 2, lat_rows, 128), f32),
            pltpu.VMEM((2, 8, lon_cols), jnp.int32),
            pltpu.VMEM((2, lat_rows, 128), jnp.int32),
            pltpu.VMEM((2, channels + 2, lon_cols), f32),
            pltpu.VMEM((lat_rows, 128), f32),
            pltpu.VMEM((lon_size - 1, slots // 2, quantities, 2 * lat_rows), f32),
            pltpu.VMEM((lon_size - 1, slots // 2, quantities, 2 * lat_rows), f32),
            pltpu.VMEM((slots, quantities, lat_rows), bf16),
            pltpu.VMEM((2 * slots, degrees), bf16),
            pltpu.VMEM((slots, quantities, lat_rows), f32),
            pltpu.VMEM((rows, 2 * slots), f32),
            pltpu.VMEM((lon_size, slots // 2, quantities, 2 * lat_rows), f32),
            pltpu.VMEM((lon_size, quantities, 2 * slots), f32),
            pltpu.VMEM((groups, rows, width), f32),
            pltpu.VMEM((groups, rows // 2, width), f32),
            pltpu.VMEM((groups, staged, width), bf16),
            pltpu.VMEM((groups, staged, width), bf16),
            pltpu.VMEM((groups, rows, width), bf16),
            dma((1,)),
            dma((2, 8)),
            dma((lon_size - 1,)),
            dma((lon_size - 1,)),
            dma((lon_size - 1, 2)),
            dma((lon_size - 1, 2)),
            dma(most),
            dma(most),
            dma(most),
            dma(most),
            dma((6,)),
            dma((6,)),
        ],
        compiler_params=pltpu.CompilerParams(
            collective_id=0, has_side_effects=True, vmem_limit_bytes=40 * 1024 * 1024
        ),
        cost_estimate=pl.CostEstimate(
            flops=4 * rows * lat_rows * degrees,
            bytes_accessed=2 * slots * lat_rows * degrees,
            transcendentals=0,
        ),
    )(parts, legendre, load[None, :], leg_edges, *fields)


def on_device(elevation, depth, friction, land_mask, order_map, legendre, load):
    channels, lat_rows, lon_cols = elevation.shape
    slot_count = legendre.shape[0]
    band_count = lax.axis_size("lat")
    sector_count = lax.axis_size("lon")
    lat_count = lat_rows * band_count
    lon_count = lon_cols * sector_count
    band = lax.axis_index("lat")
    lat_start = band * lat_rows
    col_start = lax.axis_index("lon") * lon_cols
    sea_mask = land_mask.astype(jnp.float32)

    steps = jnp.arange(lon_cols + 128, dtype=jnp.int32)
    steps = jnp.where(steps == lon_cols + 127, -1, steps)
    columns = (col_start + steps + lon_count) % lon_count
    basis = fourier_basis(order_map, columns, lon_count)
    longitude = columns.astype(jnp.float32) * (2.0 * math.pi / lon_count)
    waves = jnp.stack(
        [jnp.cos(2.0 * longitude), jnp.sin(2.0 * longitude), jnp.cos(longitude), jnp.sin(longitude)]
    )
    lines = jnp.arange(lat_rows + 8, dtype=jnp.int32)
    lines = lat_start + jnp.where(lines == lat_rows + 7, -1, lines)
    lat_step = 2.0 * LAT_EDGE / lat_count
    latitude = -LAT_EDGE + (lines.astype(jnp.float32) + 0.5) * lat_step
    face_latitude = -LAT_EDGE + (lines.astype(jnp.float32) + 1.0) * lat_step
    lat_table = jnp.stack(
        [
            jnp.cos(latitude) ** 2,
            jnp.sin(2.0 * latitude),
            1.0 / jnp.cos(latitude),
            jnp.cos(face_latitude),
        ],
        axis=1,
    )
    poles = jnp.stack([band < band_count - 1, band > 0]).astype(jnp.float32)

    leg_edges = jnp.stack([legendre[:, 0], legendre[:, -1]])
    flat_field = (elevation * sea_mask).reshape(channels * lat_rows, lon_cols)
    product = lax.dot_general(
        basis[:, :lon_cols],
        flat_field,
        (((1,), (1,)), ((), ())),
        precision=PRECISE,
        preferred_element_type=jnp.float32,
    )
    parts = product.reshape(sector_count, slot_count, 2 * channels, lat_rows)
    blocks, row_halo, col_halo = transform(
        parts,
        legendre,
        load,
        leg_edges,
        (elevation, depth, friction, land_mask),
        band_count,
        sector_count,
    )
    synth = blocks[:, :, : lat_rows + 8].reshape(-1, 2, channels, lat_rows + 8)
    synth = synth.transpose(2, 3, 0, 1).reshape(channels, lat_rows + 8, basis.shape[0])
    return tuple(
        sweep(
            elevation,
            depth,
            friction,
            land_mask,
            (row_halo, col_halo),
            synth,
            basis,
            lat_table,
            waves,
            poles,
        )
    )


def solution(mesh):
    return jax.shard_map(
        on_device,
        mesh=mesh,
        in_specs=(
            P(None, "lat", "lon"),
            P("lat", "lon"),
            P("lat", "lon"),
            P("lat", "lon"),
            P(),
            P("lon", "lat", None),
            P(),
        ),
        out_specs=(P(None, "lat", "lon"), P(None, "lat", "lon"), P("lat", "lon")),
        check_vma=False,
    )
```

```python
import functools
import math

import jax
import jax.numpy as jnp
from jax import lax
from jax.experimental import pallas as pl
from jax.experimental.pallas import tpu as pltpu
from jax.sharding import PartitionSpec as P

SAMPLES = 64


FREQUENCIES = (1.0, 1.0347, 0.9582, 1.0379, 0.5018, 0.4651, 0.4986, 0.4482)
EQ_AMPS = (0.73, 0.34, 0.14, 0.09, 0.42, 0.3, 0.14, 0.06)
LAT_EDGE = 1.3614
RELAX_RATE = 0.1
BASE_FRICTION = 0.05
DRAG_COEFF = 0.5
SPEED_EPS = 0.001
STEP_TIME = 3.0
PRECISE = lax.Precision.HIGHEST


def fourier_basis(order_map, columns, lon_count):
    product = order_map[:, None] * columns[None, :] % lon_count
    angles = product.astype(jnp.float32) * (2.0 * math.pi / lon_count)
    scaling = jnp.where(
        order_map > 0, math.sqrt(2.0 / lon_count), math.sqrt(1.0 / lon_count)
    ).astype(jnp.float32)[:, None]
    harmonics = jnp.stack([jnp.cos(angles) * scaling, jnp.sin(angles) * scaling], axis=1)
    return harmonics.reshape(2 * order_map.shape[0], columns.shape[0])


def sample_table():
    sample_time = STEP_TIME * jnp.arange(SAMPLES, dtype=jnp.float32)[:, None]
    omegas = jnp.asarray(FREQUENCIES, dtype=jnp.float32)[None, :]
    phases = sample_time * omegas
    return jnp.stack([jnp.cos(phases), jnp.sin(phases)], axis=2).reshape(
        SAMPLES, 2 * len(FREQUENCIES)
    )


def sweep_kernel(
    omega_ref,
    amp_ref,
    pole_ref,
    elev_ref,
    depth_ref,
    drag_ref,
    mask_ref,
    row_halo_ref,
    col_halo_ref,
    synth_ref,
    basis_ref,
    lat_ref,
    wave_ref,
    weight_ref,
    new_ref,
    sal_ref,
    friction_ref,
    coefs,
    east_cells,
    north_cells,
):
    k = pl.program_id(0)
    channels = 2 * pl.num_programs(0)
    lat_rows, lon_cols = depth_ref.shape
    wide_rows, wide_cols = lat_rows + 8, lon_cols + 128

    def rolled(value, shift, axis):
        return pltpu.roll(value, shift % value.shape[axis], axis)

    lane = lax.broadcasted_iota(jnp.int32, (lat_rows, 128), 1)
    line = lax.broadcasted_iota(jnp.int32, (8, lon_cols), 0)

    def widened(main, field):
        right = jnp.sum(jnp.where(lane == field, col_halo_ref[0], 0.0), axis=1, keepdims=True)
        left = jnp.sum(jnp.where(lane == 64 + field, col_halo_ref[1], 0.0), axis=1, keepdims=True)
        sides = jnp.where(lane == 0, right, jnp.where(lane == 127, left, 0.0))
        below = row_halo_ref[0, pl.ds(field, 1), :]
        above = row_halo_ref[1, pl.ds(field, 1), :]
        ends = jnp.where(line == 0, below, jnp.where(line == 7, above, 0.0))
        corner = jnp.zeros((8, 128), jnp.float32)
        return jnp.concatenate(
            [
                jnp.concatenate([main, sides], axis=1),
                jnp.concatenate([ends, corner], axis=1),
            ],
            axis=0,
        )

    inverse_cos = lat_ref[:, 2:3]
    cos_face = lat_ref[:, 3:4]

    @pl.when(k == 0)
    def _():
        depth = widened(depth_ref[...] * mask_ref[...].astype(jnp.float32), channels)
        row = lax.broadcasted_iota(jnp.int32, (wide_rows, wide_cols), 0)
        depth = jnp.where(
            row == lat_rows, depth * pole_ref[0], jnp.where(row == wide_rows - 1, depth * pole_ref[1], depth)
        )
        drag = widened(drag_ref[...], channels + 1)
        for face, axis in enumerate((1, 0)):
            square = depth * rolled(depth, -1, axis)
            mean = 0.5 * (drag + rolled(drag, -1, axis))
            coefs[4 * face] = square * mean
            coefs[4 * face + 1] = square * jnp.sqrt(square)
            coefs[4 * face + 2] = mean * mean
            coefs[4 * face + 3] = square

    omega = omega_ref[k]
    kind = k // 4
    lat_shape = amp_ref[k] * jnp.where(kind == 0, lat_ref[:, 0:1], lat_ref[:, 1:2])
    surface = []
    for part in range(2):
        sal = jnp.dot(
            synth_ref[part],
            basis_ref[...],
            precision=PRECISE,
            preferred_element_type=jnp.float32,
        )
        sal_ref[part] = sal[:lat_rows, :lon_cols]
        wave = wave_ref[pl.ds(2 * kind + part, 1), :]
        surface.append(widened(elev_ref[part], 2 * k + part) - lat_shape * wave - sal)
    divergence = [None, None]
    for face, (axis, factor, cells) in enumerate(
        ((1, inverse_cos, east_cells), (0, cos_face, north_cells))
    ):
        inverse = 1.0 / (coefs[4 * face + 2] + (omega * omega) * coefs[4 * face + 3])
        real_coef = coefs[4 * face] * inverse * factor
        imag_coef = (omega * coefs[4 * face + 1]) * inverse * factor
        diff_real = rolled(surface[0], -1, axis) - surface[0]
        diff_imag = rolled(surface[1], -1, axis) - surface[1]
        fluxes = (
            imag_coef * diff_imag - real_coef * diff_real,
            -(real_coef * diff_imag + imag_coef * diff_real),
        )
        for part, flux in enumerate(fluxes):
            back = rolled(flux, 1, axis)
            change = (flux - back)[:lat_rows, :lon_cols]
            divergence[part] = change if face == 0 else divergence[part] + change
            mean = (0.5 * (flux + back))[:lat_rows, :lon_cols]
            cells[:, pl.ds(2 * k + part, 1), :] = mean.reshape(lat_rows, 1, lon_cols)
    sea_mask = mask_ref[...].astype(jnp.float32)
    inner_cos = inverse_cos[:lat_rows]
    real, imag = elev_ref[0], elev_ref[1]
    new_ref[0] = (real - RELAX_RATE * (divergence[0] * inner_cos + omega * imag)) * sea_mask
    new_ref[1] = (imag - RELAX_RATE * (divergence[1] * inner_cos - omega * real)) * sea_mask

    @pl.when(k == pl.num_programs(0) - 1)
    def _():
        weights = weight_ref[...]
        weights_top = weights.astype(jnp.bfloat16)
        weights_rest = (weights - weights_top.astype(jnp.float32)).astype(jnp.bfloat16)
        stacked = jnp.concatenate([weights_top, weights_top, weights_rest], axis=1)

        def sampled(value):
            top = value.astype(jnp.bfloat16)
            rest = (value - top.astype(jnp.float32)).astype(jnp.bfloat16)
            return jnp.dot(
                stacked,
                jnp.concatenate([top, rest, top], axis=0),
                preferred_element_type=jnp.float32,
            )

        @pl.loop(0, lat_rows, unroll=UNROLL)
        def _(j):
            east, north = sampled(east_cells[j]), sampled(north_cells[j])
            squares = east * east + north * north + SPEED_EPS * SPEED_EPS
            speeds = squares * lax.rsqrt(squares)
            mean = jnp.sum(speeds, axis=0, keepdims=True) * (DRAG_COEFF / SAMPLES)
            friction_ref[pl.ds(j, 1), :] = BASE_FRICTION + mean


def sweep(elevation, depth, friction, land_mask, halos, synth, basis, lat_table, waves, poles):
    channels, lat_rows, lon_cols = elevation.shape
    wide_rows, wide_cols = lat_rows + 8, lon_cols + 128
    whole = pl.BlockSpec(memory_space=pltpu.VMEM)
    scalars = pl.BlockSpec(memory_space=pltpu.SMEM)

    def fixed(value):
        return pl.BlockSpec(value.shape, lambda k: (0,) * value.ndim)

    def pair(*shape):
        return pl.BlockSpec((2,) + shape, lambda k: (k, 0, 0))

    return pl.pallas_call(
        sweep_kernel,
        grid=(channels // 2,),
        out_shape=[
            jax.ShapeDtypeStruct(elevation.shape, jnp.float32),
            jax.ShapeDtypeStruct(elevation.shape, jnp.float32),
            jax.ShapeDtypeStruct(depth.shape, jnp.float32),
        ],
        in_specs=[scalars] * 3
        + [pair(lat_rows, lon_cols)]
        + [fixed(value) for value in (depth, friction, land_mask) + halos]
        + [pair(wide_rows, basis.shape[0])]
        + [fixed(basis), fixed(lat_table), fixed(waves), whole],
        out_specs=[
            pair(lat_rows, lon_cols),
            pair(lat_rows, lon_cols),
            pl.BlockSpec((lat_rows, lon_cols), lambda k: (0, 0)),
        ],
        scratch_shapes=[
            pltpu.VMEM((8, wide_rows, wide_cols), jnp.float32),
            pltpu.VMEM((lat_rows, channels, lon_cols), jnp.float32),
            pltpu.VMEM((lat_rows, channels, lon_cols), jnp.float32),
        ],
        compiler_params=pltpu.CompilerParams(
            dimension_semantics=("arbitrary",), vmem_limit_bytes=60 * 1024 * 1024
        ),
    )(
        jnp.asarray(FREQUENCIES, dtype=jnp.float32),
        jnp.asarray(EQ_AMPS, dtype=jnp.float32),
        poles,
        elevation,
        depth,
        friction,
        land_mask,
        *halos,
        synth,
        basis,
        lat_table,
        waves,
        sample_table(),
    )


GROUPS = 4
UNROLL = 16
MESH = pl.DeviceIdType.MESH


def lat_factors(lat_size):
    return (2, lat_size // 8, 4)


def transform_kernel(
    factors,
    lon_size,
    groups,
    part_ref,
    leg_hbm,
    load_ref,
    leg_edges_ref,
    elev_hbm,
    depth_hbm,
    drag_hbm,
    mask_hbm,
    out_ref,
    row_halo_ref,
    col_halo_ref,
    leg_ref,
    row_strips,
    col_strips,
    row_masks,
    col_masks,
    row_edges,
    col_edges,
    packed_out,
    packed_in,
    fourier,
    leg_halo,
    synth,
    synth_edges,
    packed_synth,
    packed_edges,
    acc,
    first_recv,
    rs_send,
    rs_recv,
    gathered,
    leg_sem,
    strip_sem,
    lon_send,
    lon_recv,
    out_send,
    out_recv,
    red_send,
    red_recv,
    gat_send,
    gat_recv,
    halo_send,
    halo_recv,
):
    lat_me = lax.axis_index("lat")
    lon_me = lax.axis_index("lon")
    lat_size = math.prod(factors)
    phases = len(factors)
    slots, lat_rows, degrees = leg_ref.shape
    quantities = part_ref.shape[2]
    channels = elev_hbm.shape[0]
    lon_cols = elev_hbm.shape[2]
    rows = slots * quantities
    width = degrees // groups
    pairs = slots // 2

    loads = [pltpu.make_async_copy(leg_hbm, leg_ref, leg_sem.at[0])]
    for side in range(2):
        top, first = side * (lat_rows - 8), side * (lon_cols - 128)
        for n, (field, row_to, col_to) in enumerate(
            (
                (elev_hbm, row_strips.at[side, :channels], col_strips.at[side, :channels]),
                (depth_hbm, row_strips.at[side, channels], col_strips.at[side, channels]),
                (drag_hbm, row_strips.at[side, channels + 1], col_strips.at[side, channels + 1]),
                (mask_hbm, row_masks.at[side], col_masks.at[side]),
            )
        ):
            lead = (slice(None),) if n == 0 else ()
            row_from = field.at[lead + (pl.ds(top, 8), slice(None))]
            col_from = field.at[lead + (slice(None), pl.ds(first, 128))]
            loads.append(pltpu.make_async_copy(row_from, row_to, strip_sem.at[side, n]))
            loads.append(pltpu.make_async_copy(col_from, col_to, strip_sem.at[side, 4 + n]))
    for copy in loads[1:] + loads[:1]:
        copy.start()

    digits, peers, kept, sizes = [], [], [0], [rows]
    stride = 1
    for factor in factors:
        digit = (lat_me // stride) % factor
        around = [(digit + d) % factor for d in range(1, factor)]
        digits.append(digit)
        peers.append([(other, lat_me + (other - digit) * stride) for other in around])
        sizes.append(sizes[-1] // factor)
        kept.append(pl.multiple_of(kept[-1] + digit * sizes[-1], sizes[-1]))
        stride *= factor
    others = [lax.rem(lon_me + d, lon_size) for d in range(1, lon_size)]
    above, below = lax.rem(lat_me + lat_size - 1, lat_size), lax.rem(lat_me + 1, lat_size)
    left, right = lax.rem(lon_me + lon_size - 1, lon_size), lax.rem(lon_me + 1, lon_size)

    barrier = pltpu.get_barrier_semaphore()
    greeted = [(other, lon_me) for phase in peers for _, other in phase]
    greeted += [(above, lon_me), (below, lon_me)] + [(lat_me, other) for other in others]
    for device in greeted:
        pl.semaphore_signal(barrier, inc=1, device_id=device, device_id_type=MESH)
    for d, other in enumerate(others):
        packed_out[d, :, :, :lat_rows] = part_ref[other, :pairs]
        packed_out[d, :, :, lat_rows:] = part_ref[other, pairs:]
    pl.semaphore_wait(barrier, len(greeted))

    pending = []

    def send(source, target, send_sem, recv_sem, device):
        copy = pltpu.make_async_remote_copy(
            src_ref=source,
            dst_ref=target,
            send_sem=send_sem,
            recv_sem=recv_sem,
            device_id=device,
            device_id_type=MESH,
        )
        copy.start()
        pending.append(copy)
        return copy

    copies = [
        send(packed_out.at[d], packed_in.at[d], lon_send.at[d], lon_recv.at[d], (lat_me, other))
        for d, other in enumerate(others)
    ]

    for copy in loads[1:]:
        copy.wait()
    lane = lax.broadcasted_iota(jnp.int32, (lat_rows, 128), 1)
    edge_cols = jnp.zeros((lat_rows, 128), jnp.float32)
    for side in range(2):
        row, col = 7 * side, 127 * side
        for field in range(channels + 2):
            line = row_strips[side, field, row : row + 1, :]
            column = col_strips[side, field, :, col : col + 1]
            if field == channels:
                line = line * row_masks[side, row : row + 1, :].astype(jnp.float32)
                column = column * col_masks[side, :, col : col + 1].astype(jnp.float32)
            row_edges[side, field : field + 1, :] = line
            edge_cols = jnp.where(lane == 64 * side + field, column, edge_cols)
    col_edges[...] = edge_cols
    halos = [
        send(source, target, halo_send.at[n], halo_recv.at[n], device)
        for n, (source, target, device) in enumerate(
            (
                (leg_edges_ref.at[0], leg_halo.at[pl.ds(0, slots)], (above, lon_me)),
                (leg_edges_ref.at[1], leg_halo.at[pl.ds(slots, slots)], (below, lon_me)),
                (row_edges.at[0], row_halo_ref.at[0], (above, lon_me)),
                (row_edges.at[1], row_halo_ref.at[1], (below, lon_me)),
                (col_edges, col_halo_ref.at[0], (lat_me, left)),
                (col_edges, col_halo_ref.at[1], (lat_me, right)),
            )
        )
    ]
    for copy in copies:
        copy.wait_recv()
    for half in range(2):
        total = part_ref[lon_me, half * pairs : (half + 1) * pairs]
        for d in range(lon_size - 1):
            total = total + packed_in[d, :, :, half * lat_rows : (half + 1) * lat_rows]
        fourier[half * pairs : (half + 1) * pairs] = total.astype(jnp.bfloat16)
    loads[0].wait()

    reducing = {}
    gathering = {}
    offsets = [0, 0]
    for p in range(1, phases):
        offsets.append(offsets[-1] + (factors[p] - 1) * sizes[p + 1])

    def analyse(g):
        @pl.loop(0, slots, unroll=UNROLL)
        def _(s):
            acc[g, pl.ds(pl.multiple_of(s * quantities, quantities), quantities), :] = jnp.dot(
                fourier[s],
                leg_ref[s, :, g * width : (g + 1) * width],
                preferred_element_type=jnp.float32,
            )

        away = pl.multiple_of(peers[0][0][0] * sizes[1], sizes[1])
        reducing[g] = [
            send(
                acc.at[g, pl.ds(away, sizes[1]), :],
                first_recv.at[g],
                red_send.at[g, 0, 0],
                red_recv.at[g, 0, 0],
                (peers[0][0][1], lon_me),
            )
        ]

    def reduce(g, p):
        for copy in reducing[g]:
            copy.wait_recv()
        size = sizes[p + 1]

        def value(start, count):
            total = acc[g, pl.ds(pl.multiple_of(kept[p + 1] + start, count), count), :]
            if p == 0:
                return total + first_recv[g, pl.ds(start, count), :]
            for d in range(factors[p] - 1):
                place = pl.multiple_of(offsets[p] + d * size + start, 16)
                total = total + rs_recv[g, pl.ds(place, count), :].astype(jnp.float32)
            return total

        if p < phases - 1:
            sub = sizes[p + 2]
            reducing[g] = []
            for d, (digit, device) in enumerate(peers[p + 1]):
                place = pl.ds(offsets[p + 1] + d * sub, sub)
                rs_send[g, place, :] = value(pl.multiple_of(digit * sub, sub), sub).astype(
                    jnp.bfloat16
                )
                reducing[g].append(
                    send(
                        rs_send.at[g, place, :],
                        rs_recv.at[g, place, :],
                        red_send.at[g, p + 1, d],
                        red_recv.at[g, p + 1, d],
                        (device, lon_me),
                    )
                )
            acc[g, pl.ds(kept[p + 2], sub), :] = value(
                pl.multiple_of(digits[p + 1] * sub, sub), sub
            )
        else:
            scale = load_ref[:, g * width : (g + 1) * width]
            gathered[g, pl.ds(kept[phases], size), :] = (value(0, size) * scale).astype(
                jnp.bfloat16
            )
            spread(g, phases - 1)

    def spread(g, p):
        held = pl.ds(kept[p + 1], sizes[p + 1])
        gathering[g] = [
            send(
                gathered.at[g, held, :],
                gathered.at[g, held, :],
                gat_send.at[g, p, d],
                gat_recv.at[g, p, d],
                (device, lon_me),
            )
            for d, (_, device) in enumerate(peers[p])
        ]

    def synthesise(g):
        if g == 0:
            for copy in halos[:2]:
                copy.wait_recv()
        at_edges = lax.dot_general(
            gathered[g],
            leg_halo[:, g * width : (g + 1) * width],
            (((1,), (1,)), ((), ())),
            preferred_element_type=jnp.float32,
        )
        if g == 0:
            synth_edges[...] = at_edges
        else:
            synth_edges[...] = synth_edges[...] + at_edges

        @pl.loop(0, slots, unroll=UNROLL)
        def _(s):
            part = lax.dot_general(
                gathered[g, pl.ds(pl.multiple_of(s * quantities, quantities), quantities), :],
                leg_ref[s, :, g * width : (g + 1) * width],
                (((1,), (1,)), ((), ())),
                preferred_element_type=jnp.float32,
            )
            if g == 0:
                synth[s] = part
            else:
                synth[s] = synth[s] + part

    def gather(g, p):
        for copy in gathering[g]:
            copy.wait_recv()
        if p > 0:
            spread(g, p - 1)
        else:
            synthesise(g)

    for wave in range(groups + 2 * phases):
        for g in reversed(range(groups)):
            stage = wave - g
            if stage == 0:
                analyse(g)
            elif 1 <= stage <= phases:
                reduce(g, stage - 1)
            elif phases < stage <= 2 * phases:
                gather(g, 2 * phases - stage)

    packed_synth[lon_me, :, :, :lat_rows] = synth[:pairs]
    packed_synth[lon_me, :, :, lat_rows:] = synth[pairs:]
    edge_lane = lax.broadcasted_iota(jnp.int32, (quantities, 2 * slots), 1) % slots
    edges = jnp.zeros((quantities, 2 * slots), jnp.float32)
    for s in range(slots):
        edges = jnp.where(
            edge_lane == s, synth_edges[s * quantities : (s + 1) * quantities, :], edges
        )
    packed_edges[lon_me] = edges
    copies = []
    for d, other in enumerate(others):
        for n, array in enumerate((packed_synth, packed_edges)):
            copies.append(
                send(
                    array.at[lon_me],
                    array.at[lon_me],
                    out_send.at[d, n],
                    out_recv.at[d, n],
                    (lat_me, other),
                )
            )
    places = lax.broadcasted_iota(jnp.int32, (quantities, out_ref.shape[2] - lat_rows), 1)

    def unpack(block):
        both = packed_edges[block]
        for s in range(slots):
            slot = block * slots + s
            half = s // pairs
            out_ref[slot, :, :lat_rows] = packed_synth[
                block, s % pairs, :, half * lat_rows : (half + 1) * lat_rows
            ]
            out_ref[slot, :, lat_rows:] = jnp.where(
                places == 0,
                both[:, s : s + 1],
                jnp.where(places == 7, both[:, slots + s : slots + s + 1], 0.0),
            )

    unpack(lon_me)
    for copy in copies + halos[2:]:
        copy.wait_recv()
    for other in others:
        unpack(other)
    for copy in pending:
        copy.wait_send()


def transform(parts, legendre, load, leg_edges, fields, lat_size, lon_size):
    slots, lat_rows, degrees = legendre.shape
    quantities = parts.shape[2]
    channels, _, lon_cols = fields[0].shape
    rows = slots * quantities
    groups = GROUPS
    width = degrees // groups
    factors = lat_factors(lat_size)
    staged, size = 0, rows // factors[0]
    for factor in factors[1:]:
        size //= factor
        staged += (factor - 1) * size
    vmem = pl.BlockSpec(memory_space=pltpu.VMEM)
    anywhere = pl.BlockSpec(memory_space=pl.ANY)
    dma = pltpu.SemaphoreType.DMA
    most = (groups, len(factors), max(factors) - 1)
    f32, bf16 = jnp.float32, jnp.bfloat16
    return pl.pallas_call(
        functools.partial(transform_kernel, factors, lon_size, groups),
        out_shape=[
            jax.ShapeDtypeStruct((lon_size * slots, quantities, 128), f32),
            jax.ShapeDtypeStruct((2, channels + 2, lon_cols), f32),
            jax.ShapeDtypeStruct((2, lat_rows, 128), f32),
        ],
        in_specs=[vmem, anywhere, vmem, vmem] + [anywhere] * 4,
        out_specs=[vmem] * 3,
        scratch_shapes=[
            pltpu.VMEM(legendre.shape, bf16),
            pltpu.VMEM((2, channels + 2, 8, lon_cols), f32),
            pltpu.VMEM((2, channels + 2, lat_rows, 128), f32),
            pltpu.VMEM((2, 8, lon_cols), jnp.int32),
            pltpu.VMEM((2, lat_rows, 128), jnp.int32),
            pltpu.VMEM((2, channels + 2, lon_cols), f32),
            pltpu.VMEM((lat_rows, 128), f32),
            pltpu.VMEM((lon_size - 1, slots // 2, quantities, 2 * lat_rows), f32),
            pltpu.VMEM((lon_size - 1, slots // 2, quantities, 2 * lat_rows), f32),
            pltpu.VMEM((slots, quantities, lat_rows), bf16),
            pltpu.VMEM((2 * slots, degrees), bf16),
            pltpu.VMEM((slots, quantities, lat_rows), f32),
            pltpu.VMEM((rows, 2 * slots), f32),
            pltpu.VMEM((lon_size, slots // 2, quantities, 2 * lat_rows), f32),
            pltpu.VMEM((lon_size, quantities, 2 * slots), f32),
            pltpu.VMEM((groups, rows, width), f32),
            pltpu.VMEM((groups, rows // 2, width), f32),
            pltpu.VMEM((groups, staged, width), bf16),
            pltpu.VMEM((groups, staged, width), bf16),
            pltpu.VMEM((groups, rows, width), bf16),
            dma((1,)),
            dma((2, 8)),
            dma((lon_size - 1,)),
            dma((lon_size - 1,)),
            dma((lon_size - 1, 2)),
            dma((lon_size - 1, 2)),
            dma(most),
            dma(most),
            dma(most),
            dma(most),
            dma((6,)),
            dma((6,)),
        ],
        compiler_params=pltpu.CompilerParams(
            collective_id=0, has_side_effects=True, vmem_limit_bytes=60 * 1024 * 1024
        ),
        cost_estimate=pl.CostEstimate(
            flops=4 * rows * lat_rows * degrees,
            bytes_accessed=2 * slots * lat_rows * degrees,
            transcendentals=0,
        ),
    )(parts, legendre, load[None, :], leg_edges, *fields)


def on_device(elevation, depth, friction, land_mask, order_map, legendre, load):
    channels, lat_rows, lon_cols = elevation.shape
    slot_count = legendre.shape[0]
    band_count = lax.axis_size("lat")
    sector_count = lax.axis_size("lon")
    lat_count = lat_rows * band_count
    lon_count = lon_cols * sector_count
    band = lax.axis_index("lat")
    lat_start = band * lat_rows
    col_start = lax.axis_index("lon") * lon_cols
    sea_mask = land_mask.astype(jnp.float32)

    steps = jnp.arange(lon_cols + 128, dtype=jnp.int32)
    steps = jnp.where(steps == lon_cols + 127, -1, steps)
    columns = (col_start + steps + lon_count) % lon_count
    basis = fourier_basis(order_map, columns, lon_count)
    longitude = columns.astype(jnp.float32) * (2.0 * math.pi / lon_count)
    waves = jnp.stack(
        [jnp.cos(2.0 * longitude), jnp.sin(2.0 * longitude), jnp.cos(longitude), jnp.sin(longitude)]
    )
    lines = jnp.arange(lat_rows + 8, dtype=jnp.int32)
    lines = lat_start + jnp.where(lines == lat_rows + 7, -1, lines)
    lat_step = 2.0 * LAT_EDGE / lat_count
    latitude = -LAT_EDGE + (lines.astype(jnp.float32) + 0.5) * lat_step
    face_latitude = -LAT_EDGE + (lines.astype(jnp.float32) + 1.0) * lat_step
    lat_table = jnp.stack(
        [
            jnp.cos(latitude) ** 2,
            jnp.sin(2.0 * latitude),
            1.0 / jnp.cos(latitude),
            jnp.cos(face_latitude),
        ],
        axis=1,
    )
    poles = jnp.stack([band < band_count - 1, band > 0]).astype(jnp.float32)

    leg_edges = jnp.stack([legendre[:, 0], legendre[:, -1]])
    flat_field = (elevation * sea_mask).reshape(channels * lat_rows, lon_cols)
    product = lax.dot_general(
        basis[:, :lon_cols],
        flat_field,
        (((1,), (1,)), ((), ())),
        precision=PRECISE,
        preferred_element_type=jnp.float32,
    )
    parts = product.reshape(sector_count, slot_count, 2 * channels, lat_rows)
    blocks, row_halo, col_halo = transform(
        parts,
        legendre,
        load,
        leg_edges,
        (elevation, depth, friction, land_mask),
        band_count,
        sector_count,
    )
    synth = blocks[:, :, : lat_rows + 8].reshape(-1, 2, channels, lat_rows + 8)
    synth = synth.transpose(2, 3, 0, 1).reshape(channels, lat_rows + 8, basis.shape[0])
    return tuple(
        sweep(
            elevation,
            depth,
            friction,
            land_mask,
            (row_halo, col_halo),
            synth,
            basis,
            lat_table,
            waves,
            poles,
        )
    )


def solution(mesh):
    return jax.shard_map(
        on_device,
        mesh=mesh,
        in_specs=(
            P(None, "lat", "lon"),
            P("lat", "lon"),
            P("lat", "lon"),
            P("lat", "lon"),
            P(),
            P("lon", "lat", None),
            P(),
        ),
        out_specs=(P(None, "lat", "lon"), P(None, "lat", "lon"), P("lat", "lon")),
        check_vma=False,
    )
```
